768 devices in a mesh: slab: 192 (over z, y_lo, x, core), col: 4 (over y_hi).
Axes of the slice: x: 4, y: 8 (y_hi: 4, y_lo: 2; y = y_hi * 2 + y_lo), z: 12, core: 2. Of those that a mesh axis runs over, the one named last changes fastest.
Arguments:
- density: float32 [384, 128, 256], P('slab', 'col'), may hold values from 0.5 to 2
- velocity: float32 [3, 384, 128, 256], P(None, 'slab', 'col'), may hold values from -3 to 3
- pressure: float32 [384, 128, 256], P('slab', 'col'), may hold values from 0.5 to 2
- fraction_code: int32 [384, 128, 256], P('slab', 'col'), may hold values from 8 to 16
- interface_cell: int32 [192, 4, 512], P('slab', 'col'), may hold values from 0 to 16383
- interface_element: int32 [192, 4, 512], P('slab', 'col'), may hold values from 0 to 511
- interface_count: int32 [192, 4], P('slab', 'col'), may hold values from 64 to 512, as said below
- wall_normal: float32 [3, 192, 4, 512], P(None, 'slab', 'col'), may hold values from -4 to 4
- element_mass: float32 [192, 512], P('slab'), may hold values from 0.5 to 2
- element_removed: int32 [192, 512], P('slab'), may hold values 0 or 1
- element_velocity: float32 [3, 192, 512], P(None, 'slab'), may hold values from -3 to 3
Outputs:
- new_state: float32 [5, 384, 128, 256], P(None, 'slab', 'col')
- new_velocity: float32 [3, 192, 512], P(None, 'slab', 'col')
The draws below stay inside these ranges and needn't reach their ends.
Inputs may be any that keep to these rules, and one draw needn't show every extreme that they name: `interface_cell`: index within the block of 2 x 32 x 256 cells of its slab and column. `interface_element`: element of the row's own slab group. `interface_count`: each count is 512, 256, 128 or 64; some slab and column has 512.
All inputs are finite; a program needn't handle non-finite values. No bound on the sum of `element_removed` on one device may be relied on, other than what follows from the above.
Results may differ from the reference program's by a relative error of at most 0.0003.
Values sent between devices are 32-bit elements; how exact they have to be, the bound alone decides.
No kernel may reach another device: no remote copies, remote signals or barrier semaphores. Data moves between devices by JAX's collectives and lax.ppermute only.
A program may use at most 64 MiB of HBM per device.

```python
import math
import jax
import jax.numpy as jnp
from jax import lax

CX = 2
CY = 32
CZ = 256
I_DEV = 512
SLABS = 192
COLS = 4
NX = 384
NY = 128
E_GRP = 512


def draw_interface_count(key, part):
    key_one, key_two = jax.random.split(key)
    levels = jax.random.randint(key_one, (SLABS, COLS), 0, 4)
    counts = I_DEV // jnp.left_shift(jnp.ones_like(levels), levels)
    chosen_spot = jax.random.randint(key_two, (), 0, SLABS * COLS)
    flattened = counts.reshape(-1).at[chosen_spot].set(I_DEV)
    return flattened.reshape(SLABS, COLS).astype(jnp.int32)


def place_ends(drawn, rng, least, largest):
    place = [jax.random.randint(jax.random.fold_in(rng, axis), (), 0, length) for axis, length in enumerate(drawn.shape)]
    longest = drawn.shape.index(max(drawn.shape))
    neighbour = place[:longest] + [(place[longest] + 1) % drawn.shape[longest]] + place[longest + 1:]
    return drawn.at[tuple(place)].set(least).at[tuple(neighbour)].set(largest)


def block_scale(key, shape, shards, least, high):
    factor_of, own = 1.0, jax.random.fold_in(key, 6)
    for dim, parts in shards:
        heights = jnp.exp(jax.random.uniform(jax.random.fold_in(own, dim), (parts,), jnp.float32, least / len(shards), high / len(shards)))
        factor_of = factor_of * jnp.repeat(heights, shape[dim] // parts).reshape([-1 if axis == dim else 1 for axis in range(len(shape))])
    return factor_of


def centred(own_key, shape, deviation, most, pieces=(), held_as=jnp.bfloat16):
    gain = block_scale(own_key, shape, pieces, -0.22, 0.18) if pieces else 1.0
    values = jax.random.normal(own_key, shape, jnp.float32) * deviation * gain
    return jnp.minimum(jnp.maximum(values, -most), most).astype(held_as)


def setup_inputs(seed: int = 0) -> dict:
    arg_keys = jax.random.split(jax.random.key(seed), 12)
    density = jnp.clip(jnp.exp(math.log(2.0) - 1.3862944 * jax.random.uniform(arg_keys[0], (NX, NY, CZ), jnp.float32) ** block_scale(arg_keys[0], (NX, NY, CZ), ((0, 192), (1, 4)), -0.2, 0.2)), 0.5, 2.0)
    velocity = centred(arg_keys[1], (3, NX, NY, CZ), 0.5, 3.0, ((1, 192), (2, 4)), jnp.float32)
    pressure = jnp.clip(jnp.exp(math.log(2.0) - 1.3862944 * jax.random.uniform(arg_keys[2], (NX, NY, CZ), jnp.float32) ** block_scale(arg_keys[2], (NX, NY, CZ), ((0, 192), (1, 4)), -0.2, 0.2)), 0.5, 2.0)
    fraction_code = place_ends(jax.random.randint(arg_keys[3], (NX, NY, CZ), 8, 17), jax.random.fold_in(arg_keys[3], 1), 8, 16).astype(jnp.int32)
    interface_cell = place_ends(jax.random.randint(arg_keys[4], (SLABS, COLS, I_DEV), 0, CX * CY * CZ), jax.random.fold_in(arg_keys[4], 1), 0, (CX * CY * CZ) - 1).astype(jnp.int32)
    interface_element = place_ends(jax.random.randint(arg_keys[5], (SLABS, COLS, I_DEV), 0, E_GRP), jax.random.fold_in(arg_keys[5], 1), 0, E_GRP - 1).astype(jnp.int32)
    interface_count = draw_interface_count(jax.random.fold_in(arg_keys[11], 71), 0)
    wall_normal = centred(arg_keys[7], (3, SLABS, COLS, I_DEV), 1.0, 4.0, ((1, 192), (2, 4)), jnp.float32)
    element_mass = jnp.clip(jnp.exp(math.log(2.0) - 1.3862944 * jax.random.uniform(arg_keys[8], (SLABS, E_GRP), jnp.float32) ** block_scale(arg_keys[8], (SLABS, E_GRP), ((0, 192),), -0.2, 0.2)), 0.5, 2.0)
    element_removed = place_ends((jax.random.randint(arg_keys[9], (SLABS, E_GRP), 0, 4) < 1).astype(jnp.int32), jax.random.fold_in(arg_keys[9], 1), 0, 1)
    element_velocity = centred(arg_keys[10], (3, SLABS, E_GRP), 0.5, 3.0, ((1, 192),), jnp.float32)
    return {"density": density, "velocity": velocity, "pressure": pressure, "fraction_code": fraction_code, "interface_cell": interface_cell, "interface_element": interface_element, "interface_count": interface_count, "wall_normal": wall_normal, "element_mass": element_mass, "element_removed": element_removed, "element_velocity": element_velocity}


ratio_heat = 1.4
step_ratio = 0.1
struct_step = 1.0

def cell_terms(density_s, velocity_s, pressure_s, along):
    normal = velocity_s[along]
    energy = pressure_s / (ratio_heat - 1.0) + 0.5 * density_s * (velocity_s[0] * velocity_s[0] + velocity_s[1] * velocity_s[1] + velocity_s[2] * velocity_s[2])
    conserved = jnp.stack([density_s, density_s * velocity_s[0], density_s * velocity_s[1], density_s * velocity_s[2], energy])
    zero_plane = jnp.zeros_like(pressure_s)
    pressure_terms = [zero_plane, zero_plane, zero_plane, zero_plane, pressure_s * normal]
    pressure_terms[1 + along] = pressure_s
    flux_terms = normal[None] * conserved + jnp.stack(pressure_terms)
    wave_speed = jnp.abs(normal) + jnp.sqrt(ratio_heat * pressure_s / density_s)
    return (conserved, flux_terms, wave_speed)

def cut_range(array, start, stop, along):
    return lax.slice_in_dim(array, start, stop, axis=array.ndim - 3 + along)

def face_sum(conserved, flux_terms, wave_speed, fraction, along):
    extent = fraction.shape[along]

    def take_low(array):
        return cut_range(array, 0, extent - 1, along)

    def take_high(array):
        return cut_range(array, 1, extent, along)
    face_flux = 0.5 * (take_low(flux_terms) + take_high(flux_terms)) - 0.5 * jnp.maximum(take_low(wave_speed), take_high(wave_speed))[None] * (take_high(conserved) - take_low(conserved))
    weighted = jnp.minimum(take_low(fraction), take_high(fraction))[None] * face_flux
    return cut_range(weighted, 1, extent - 1, along) - cut_range(weighted, 0, extent - 2, along)

def interior(array, along):
    for other in range(3):
        if other != along:
            array = cut_range(array, 1, array.shape[array.ndim - 3 + other] - 1, other)
    return array

def divergence(density_p, velocity_p, pressure_p, fraction_p):
    live = fraction_p > 0.0
    density_s = jnp.where(live, density_p, 1.0)
    pressure_s = jnp.where(live, pressure_p, 1.0)
    summed = 0.0
    for along in range(3):
        conserved, flux_terms, wave_speed = cell_terms(interior(density_s, along), interior(velocity_p, along), interior(pressure_s, along), along)
        summed = summed + face_sum(conserved, flux_terms, wave_speed, interior(fraction_p, along), along)
    return summed

def reference(density, velocity, pressure, fraction_code, interface_cell, interface_element, interface_count, wall_normal, element_mass, element_removed, element_velocity):
    fraction = fraction_code.astype(jnp.float32) / 16.0
    slab_ids = jnp.arange(SLABS, dtype=jnp.int32)[:, None, None]
    column_ids = jnp.arange(COLS, dtype=jnp.int32)[None, :, None]
    plane_x = slab_ids * CX + interface_cell // (CY * CZ)
    plane_y = column_ids * CY + interface_cell // CZ % CY
    plane_z = interface_cell % CZ
    row_pressure = pressure[plane_x, plane_y, plane_z]
    row_fraction = fraction[plane_x, plane_y, plane_z]
    active = (jnp.arange(I_DEV, dtype=jnp.int32)[None, None, :] < interface_count[:, :, None]).astype(jnp.float32)
    weight = row_pressure * (1.0 - row_fraction) * active
    wall_force = -weight[None] * wall_normal
    segment_ids = (interface_element + slab_ids * E_GRP).reshape(-1)
    elem_loads = jax.ops.segment_sum(wall_force.reshape(3, -1).T, segment_ids, num_segments=SLABS * E_GRP).T.reshape(3, SLABS, E_GRP)
    keep_factor = 1.0 - element_removed.astype(jnp.float32)
    new_velocity = (element_velocity + struct_step * elem_loads / element_mass[None]) * keep_factor[None]
    row_motion = new_velocity[:, slab_ids, interface_element]
    wall_work = weight * lax.optimization_barrier(jnp.sum(wall_normal * row_motion, axis=0))
    row_terms = jnp.concatenate([weight[None] * wall_normal, wall_work[None]], axis=0)
    local_flat = interface_cell // (CY * CZ) * (NY * CZ) + plane_y * CZ + plane_z

    def one_slab(slab_pos):
        planes = slab_pos * CX - 1 + jnp.arange(CX + 2, dtype=jnp.int32)
        inside = (planes >= 0) & (planes < NX)
        clipped = jnp.clip(planes, 0, NX - 1)
        edge_pad = ((0, 0), (1, 1), (1, 1))
        fraction_p = jnp.pad(jnp.where(inside[:, None, None], jnp.take(fraction, clipped, axis=0), 0.0), edge_pad)
        density_p = jnp.pad(jnp.take(density, clipped, axis=0), edge_pad)
        pressure_p = jnp.pad(jnp.take(pressure, clipped, axis=0), edge_pad)
        velocity_p = jnp.pad(jnp.take(velocity, clipped, axis=1), ((0, 0),) + edge_pad)
        summed = divergence(density_p, velocity_p, pressure_p, fraction_p)
        centre = cell_terms(density_p[1:-1, 1:-1, 1:-1], velocity_p[:, 1:-1, 1:-1, 1:-1], pressure_p[1:-1, 1:-1, 1:-1], 0)[0]
        slab_rows = lax.dynamic_index_in_dim(row_terms, slab_pos, axis=1, keepdims=False).reshape(4, -1)
        slab_cells = lax.dynamic_index_in_dim(local_flat, slab_pos, axis=0, keepdims=False).reshape(-1)
        source = jnp.zeros((4, CX * NY * CZ), jnp.float32).at[:, slab_cells].add(slab_rows)
        source = jnp.concatenate([jnp.zeros((1, CX * NY * CZ), jnp.float32), source], axis=0).reshape(5, CX, NY, CZ)
        return centre - step_ratio / fraction_p[1:-1, 1:-1, 1:-1][None] * (summed - source)
    blocks = lax.map(one_slab, jnp.arange(SLABS, dtype=jnp.int32))
    new_state = jnp.transpose(blocks, (1, 0, 2, 3, 4)).reshape(5, NX, NY, CZ)
    return (new_state, new_velocity)
```

```python
import jax
import jax.numpy as jnp
from jax import lax
from jax.experimental import pallas as pl
from jax.experimental.pallas import tpu as pltpu
from jax.sharding import PartitionSpec as P

ratio_heat = 1.4
step_ratio = 0.1
struct_step = 1.0

F32, BF16, I32 = jnp.float32, jnp.bfloat16, jnp.int32
TILE = 8
LOADS_AT = 16


def split3(value):
    high = value.astype(BF16).astype(F32)
    rest = value - high
    middle = rest.astype(BF16).astype(F32)
    return high, middle, rest - middle


def stack_rows(rows, total):
    index = lax.broadcasted_iota(I32, (total, rows[0].shape[1]), 0)
    out = jnp.zeros((total, rows[0].shape[1]), F32)
    for at, row in enumerate(rows):
        out = jnp.where(index == at, row, out)
    return out


def gather_kernel(count_in, cell_in, element_in, *refs):
    given, kept = refs[:8], refs[8:16]
    near_ref, far_ref, message, weight_ref, third_hot, plane_hot, element_hot = refs[16:23]
    count, cell, element, sems = refs[23:]
    density, velocity, pressure, code, normal = kept[:5]
    pairs = [(cell_in, cell), (element_in, element), (count_in, count)] + list(zip(given, kept))
    copies = [pltpu.make_async_copy(a, b, sems.at[i]) for i, (a, b) in enumerate(pairs)]
    for copy in copies:
        copy.start()
    for copy in copies:
        copy.wait()
    block_x, block_y, block_z = density.shape
    rows = cell.shape[2]
    group = element_hot.shape[0]
    odd = lax.rem(lax.axis_index("slab"), 2)
    col = lax.axis_index("col")

    for target, at in ((near_ref, 1 - odd), (far_ref, odd)):
        target[0] = density[at]
        for k in range(3):
            target[1 + k] = velocity[k, at]
        target[4] = pressure[at]
        target[5] = code[at].astype(F32) * (1.0 / 16.0)

    def edge(x, y):
        out = [density[x, y : y + 1]]
        out += [velocity[k, x, y : y + 1] for k in range(3)]
        out += [pressure[x, y : y + 1], code[x, y : y + 1].astype(F32) * (1.0 / 16.0)]
        return out

    for x in range(block_x):
        first, last = edge(x, 0), edge(x, block_y - 1)
        for j in range(message.shape[0]):
            for f in range(6):
                at = f * block_x + x
                message[j, at : at + 1] = jnp.where(col < j, last[f], first[f])

    fraction = code[...].astype(F32) * (1.0 / 16.0)
    table = (pressure[...] * (1.0 - fraction)).reshape(block_x * block_y, block_z)
    place = cell[0]
    third = jnp.bitwise_and(place, block_z - 1)
    plane = lax.shift_right_logical(place, block_z.bit_length() - 1)
    third_mask = lax.broadcasted_iota(I32, (block_z, rows), 0) == third
    third_hot[...] = jnp.where(third_mask, 1.0, 0.0).astype(BF16)
    plane_mask = lax.broadcasted_iota(I32, (block_x * block_y, rows), 0) == plane
    plane_hot[...] = jnp.where(plane_mask, 1.0, 0.0).astype(BF16)
    element_mask = lax.broadcasted_iota(I32, (group, rows), 0) == element[0]
    element_hot[...] = jnp.where(element_mask, 1.0, 0.0).astype(BF16)
    parts = jnp.concatenate(split3(table), axis=0).astype(BF16)
    found = jnp.dot(parts, third_hot[...], preferred_element_type=F32)
    n = block_x * block_y
    found = found[:n] + found[n : 2 * n] + found[2 * n :]
    found = jnp.sum(jnp.where(plane_mask, found, 0.0), axis=0, keepdims=True)
    live = lax.broadcasted_iota(I32, (1, rows), 1) < count[...]
    weight = jnp.where(live, found, 0.0)
    weight_ref[...] = weight

    split = [split3(-weight * normal[k, 0]) for k in range(3)]
    force = stack_rows([split[k][i] for i in range(3) for k in range(3)], 16).astype(BF16)
    partial = lax.dot_general(
        force, element_hot[...], (((1,), (1,)), ((), ())), preferred_element_type=F32
    )
    half = group // 2
    for k in range(3):
        total = partial[k : k + 1] + partial[3 + k : 4 + k] + partial[6 + k : 7 + k]
        for h in range(2):
            at = LOADS_AT + 2 * k + h
            for j in range(message.shape[0]):
                message[j, at : at + 1] = total[:, h * half : (h + 1) * half]


def derive(density, v0, v1, v2, pressure):
    m0, m1, m2 = density * v0, density * v1, density * v2
    energy = pressure * (1.0 / 0.4) + 0.5 * density * (v0 * v0 + v1 * v1 + v2 * v2)
    sound = jnp.sqrt(ratio_heat * pressure / density)
    return m0, m1, m2, energy, sound


RHO, V0, V1, V2, PRS, FRAC, M0, M1, M2, ENE, SND = range(11)


def face(along, low, high):
    vl, vh = low[V0 + along], high[V0 + along]
    speed = jnp.maximum(jnp.abs(vl) + low[SND], jnp.abs(vh) + high[SND])
    half = 0.5 * jnp.minimum(low[FRAC], high[FRAC])
    out = []
    for i, name in enumerate((RHO, M0, M1, M2, ENE)):
        if name == RHO:
            both = low[M0 + along] + high[M0 + along]
        elif name == ENE:
            both = vl * (low[ENE] + low[PRS]) + vh * (high[ENE] + high[PRS])
        else:
            both = vl * low[name] + vh * high[name]
            if i == 1 + along:
                both = both + (low[PRS] + high[PRS])
        out.append(half * (both - speed * (high[name] - low[name])))
    return out


def step_kernel(
    density,
    velocity,
    pressure,
    code,
    normal,
    mass,
    removed,
    motion,
    near_ref,
    far_ref,
    message,
    weight_ref,
    third_hot,
    plane_hot,
    element_hot,
    state_out,
    motion_out,
    cells,
    source,
    state,
    own_motion,
    state_sem,
    motion_sem,
):
    block_x, block_y, block_z = density.shape
    group = mass.shape[1]
    share = motion_out.shape[2]
    cols = message.shape[0]
    odd = lax.rem(lax.axis_index("slab"), 2)
    col = lax.axis_index("col")
    half = group // 2
    pad = TILE

    keep = 1.0 - removed[...].astype(F32)
    new = []
    for k in range(3):
        at = LOADS_AT + 2 * k
        load = message[0, at : at + 2]
        for j in range(1, cols):
            load = load + message[j, at : at + 2]
        load = jnp.concatenate([load[0:1], load[1:2]], axis=1)
        new.append((motion[k] + struct_step * load / mass[...]) * keep)
        own = new[k][:, 0:share]
        for j in range(1, cols):
            own = jnp.where(col == j, new[k][:, j * share : (j + 1) * share], own)
        own_motion[k] = own
    motion_copy = pltpu.make_async_copy(own_motion, motion_out, motion_sem)
    motion_copy.start()
    split = [split3(value) for value in new]
    stacked = stack_rows([split[k][i] for i in range(3) for k in range(3)], 16).astype(BF16)
    moved = jnp.dot(stacked, element_hot[...], preferred_element_type=F32)
    weight = weight_ref[...]
    work = jnp.zeros_like(weight)
    values = []
    for k in range(3):
        row = moved[k : k + 1] + moved[3 + k : 4 + k] + moved[6 + k : 7 + k]
        work = work + normal[k, 0] * row
        values.append(weight * normal[k, 0])
    values.append(weight * work)
    hot = plane_hot[...]
    parts = [split3(value) for value in values]
    for k in range(4):
        left = jnp.concatenate([hot * parts[k][i].astype(BF16) for i in range(3)], axis=0)
        found = lax.dot_general(
            left, third_hot[...], (((1,), (1,)), ((), ())), preferred_element_type=F32
        )
        n = block_x * block_y
        source[k] = (found[:n] + found[n : 2 * n] + found[2 * n :]).reshape(
            block_x, block_y, block_z
        )

    def store(plane, at, count, prims, fraction):
        full = list(prims) + [fraction] + list(derive(*prims))
        for name, value in enumerate(full):
            cells[name, plane, at : at + count] = value

    for x in range(block_x):
        for t in range(block_y // TILE):
            at = slice(t * TILE, (t + 1) * TILE)
            prims = [density[x, at]] + [velocity[k, x, at] for k in range(3)] + [pressure[x, at]]
            store(1 + x, pad + t * TILE, TILE, prims, code[x, at].astype(F32) * (1.0 / 16.0))
    for ref, plane in ((near_ref, 3 * (1 - odd)), (far_ref, 3 * odd)):
        for t in range(block_y // TILE):
            at = slice(t * TILE, (t + 1) * TILE)
            fraction = ref[5, at]
            live = fraction > 0.0
            prims = [jnp.where(live, ref[0, at], 1.0)] + [ref[1 + k, at] for k in range(3)]
            prims.append(jnp.where(live, ref[4, at], 1.0))
            store(plane, pad + t * TILE, TILE, prims, fraction)
    for other, inside, at in (
        (jnp.maximum(col - 1, 0), col > 0, pad - 1),
        (jnp.minimum(col + 1, cols - 1), col < cols - 1, pad + block_y),
    ):
        for x in range(block_x):
            prims = [message[other, f * block_x + x][None] for f in range(5)]
            fraction = message[other, 5 * block_x + x][None]
            store(1 + x, at, 1, prims, jnp.where(inside, fraction, 0.0))

    lane = lax.broadcasted_iota(I32, (TILE, block_z), 1)
    row = lax.broadcasted_iota(I32, (TILE, block_z), 0)

    def load(plane, at, along):
        out = {}
        for name in (RHO, V0 + along, PRS, FRAC, M0, M1, M2, ENE, SND):
            out[name] = cells[name, plane, at : at + TILE]
        return out

    for x in range(block_x):
        before = None
        for t in range(-1, block_y // TILE):
            at = pad + t * TILE
            upper = face(1, load(1 + x, at, 1), load(1 + x, at + 1, 1))
            turned = [pltpu.roll(value, 1, 0) for value in upper]
            if t < 0:
                before = turned
                continue
            total = [
                value - jnp.where(row == 0, old, fresh)
                for value, old, fresh in zip(upper, before, turned)
            ]
            before = turned
            own = load(1 + x, at, 2)
            right = {name: pltpu.roll(value, block_z - 1, 1) for name, value in own.items()}
            right[FRAC] = jnp.where(lane == block_z - 1, 0.0, right[FRAC])
            upper = face(2, own, right)
            total = [
                value + (flux - pltpu.roll(flux, 1, 1)) for value, flux in zip(total, upper)
            ]
            own = load(1 + x, at, 0)
            upper = face(0, own, load(2 + x, at, 0))
            lower = face(0, load(x, at, 0), own)
            total = [value + (u - v) for value, u, v in zip(total, upper, lower)]
            scale = step_ratio / own[FRAC]
            rows = slice(t * TILE, (t + 1) * TILE)
            for i, name in enumerate((RHO, M0, M1, M2, ENE)):
                change = total[i] - source[i - 1, x, rows] if i else total[i]
                state[i, x, rows] = own[name] - scale * change
        pltpu.make_async_copy(state.at[:, x], state_out.at[:, x], state_sem.at[x]).start()
    for x in range(block_x):
        pltpu.make_async_copy(state.at[:, x], state_out.at[:, x], state_sem.at[x]).wait()
    motion_copy.wait()


def in_vmem(*arrays):
    return [pltpu.with_memory_space_constraint(array, pltpu.VMEM) for array in arrays]


def local(
    density,
    velocity,
    pressure,
    fraction_code,
    interface_cell,
    interface_element,
    interface_count,
    wall_normal,
    element_mass,
    element_removed,
    element_velocity,
):
    block_x, block_y, block_z = density.shape
    rows = interface_cell.shape[2]
    group = element_mass.shape[1]
    slabs, cols = lax.axis_size("slab"), lax.axis_size("col")
    share = group // cols
    vmem = pl.BlockSpec(memory_space=pltpu.VMEM)
    hbm = pl.BlockSpec(memory_space=pltpu.HBM)
    given = (
        density,
        velocity,
        pressure,
        fraction_code,
        wall_normal,
        element_mass,
        element_removed,
        element_velocity,
    )
    results = pl.pallas_call(
        gather_kernel,
        out_shape=tuple(pltpu.VMEM(array.shape, array.dtype) for array in given)
        + (
            pltpu.VMEM((6, block_y, block_z), F32),
            pltpu.VMEM((6, block_y, block_z), F32),
            pltpu.VMEM((cols, 24, block_z), F32),
            pltpu.VMEM((1, rows), F32),
            pltpu.VMEM((block_z, rows), BF16),
            pltpu.VMEM((block_x * block_y, rows), BF16),
            pltpu.VMEM((group, rows), BF16),
        ),
        in_specs=[pl.BlockSpec(memory_space=pl.ANY)] + [hbm] * 10,
        out_specs=[vmem] * 15,
        scratch_shapes=[
            pltpu.VMEM(interface_count.shape, I32),
            pltpu.VMEM(interface_cell.shape, I32),
            pltpu.VMEM(interface_element.shape, I32),
            pltpu.SemaphoreType.DMA((11,)),
        ],
        name="gather_rows",
    )(
        interface_count,
        interface_cell,
        interface_element,
        *given,
    )
    kept, (near, far, message), hots = results[:8], results[8:11], results[11:]

    inner = [(i, i ^ 1) for i in range(slabs)]
    outer = [(i, i + 1 if i % 2 else i - 1) for i in range(1, slabs - 1)]
    near_in = lax.ppermute(near, "slab", inner)
    far_in = lax.ppermute(far, "slab", outer)
    message_in = lax.all_to_all(message, "col", 0, 0)

    state, new_motion = pl.pallas_call(
        step_kernel,
        out_shape=(
            jax.ShapeDtypeStruct((5, block_x, block_y, block_z), F32),
            jax.ShapeDtypeStruct((3, 1, share), F32),
        ),
        in_specs=[vmem] * 15,
        out_specs=[hbm, hbm],
        scratch_shapes=[
            pltpu.VMEM((11, block_x + 2, block_y + 2 * TILE, block_z), F32),
            pltpu.VMEM((4, block_x, block_y, block_z), F32),
            pltpu.VMEM((5, block_x, block_y, block_z), F32),
            pltpu.VMEM((3, 1, share), F32),
            pltpu.SemaphoreType.DMA((block_x,)),
            pltpu.SemaphoreType.DMA,
        ],
        name="step_cells",
    )(*in_vmem(*kept, near_in, far_in, message_in, *hots))
    return (state, new_motion)


def solution(mesh):
    placed = (
        P("slab", "col", None),
        P(None, "slab", "col", None),
        P("slab", "col", None),
        P("slab", "col", None),
        P("slab", "col", None),
        P("slab", "col", None),
        P("slab", "col"),
        P(None, "slab", "col", None),
        P("slab", None),
        P("slab", None),
        P(None, "slab", None),
    )
    return jax.shard_map(
        local,
        mesh=mesh,
        in_specs=placed,
        out_specs=(P(None, "slab", "col", None), P(None, "slab", "col")),
        check_vma=False,
    )
```

```python
import jax
import jax.numpy as jnp
from jax import lax
from jax.experimental import pallas as pl
from jax.experimental.pallas import tpu as pltpu
from jax.sharding import PartitionSpec as P

ratio_heat = 1.4
step_ratio = 0.1
struct_step = 1.0

F32, BF16, I32 = jnp.float32, jnp.bfloat16, jnp.int32
TILE = 8
LOADS_AT = 16


def split3(value):
    high = value.astype(BF16).astype(F32)
    rest = value - high
    middle = rest.astype(BF16).astype(F32)
    return high, middle, rest - middle


def stack_rows(rows, total):
    index = lax.broadcasted_iota(I32, (total, rows[0].shape[1]), 0)
    out = jnp.zeros((total, rows[0].shape[1]), F32)
    for at, row in enumerate(rows):
        out = jnp.where(index == at, row, out)
    return out


def gather_kernel(count_in, cell_in, element_in, *refs):
    given, kept = refs[:8], refs[8:16]
    far_ref, near_ref, message, weight_ref, third_hot, plane_hot, element_hot = refs[16:23]
    count, cell, element, sems = refs[23:]
    density, velocity, pressure, code, normal = kept[:5]
    pairs = [(cell_in, cell), (element_in, element), (count_in, count)] + list(zip(given, kept))
    copies = [pltpu.make_async_copy(a, b, sems.at[i]) for i, (a, b) in enumerate(pairs)]
    for copy in copies:
        copy.start()
    for copy in copies:
        copy.wait()
    block_x, block_y, block_z = density.shape
    rows = cell.shape[2]
    group = element_hot.shape[0]
    odd = lax.rem(lax.axis_index("slab"), 2)
    col = lax.axis_index("col")

    for target, at in ((far_ref, odd), (near_ref, 1 - odd)):
        target[0] = density[at]
        for k in range(3):
            target[1 + k] = velocity[k, at]
        target[4] = pressure[at]
        target[5] = code[at].astype(F32) * (1.0 / 16.0)

    def edge(x, y):
        out = [density[x, y : y + 1]]
        out += [velocity[k, x, y : y + 1] for k in range(3)]
        out += [pressure[x, y : y + 1], code[x, y : y + 1].astype(F32) * (1.0 / 16.0)]
        return out

    for x in range(block_x):
        first, last = edge(x, 0), edge(x, block_y - 1)
        for j in range(message.shape[0]):
            for f in range(6):
                at = f * block_x + x
                message[j, at : at + 1] = jnp.where(col < j, last[f], first[f])

    fraction = code[...].astype(F32) * (1.0 / 16.0)
    table = (pressure[...] * (1.0 - fraction)).reshape(block_x * block_y, block_z)
    place = cell[0]
    third = jnp.bitwise_and(place, block_z - 1)
    plane = lax.shift_right_logical(place, block_z.bit_length() - 1)
    third_mask = lax.broadcasted_iota(I32, (block_z, rows), 0) == third
    third_hot[...] = jnp.where(third_mask, 1.0, 0.0).astype(BF16)
    plane_mask = lax.broadcasted_iota(I32, (block_x * block_y, rows), 0) == plane
    plane_hot[...] = jnp.where(plane_mask, 1.0, 0.0).astype(BF16)
    element_mask = lax.broadcasted_iota(I32, (group, rows), 0) == element[0]
    element_hot[...] = jnp.where(element_mask, 1.0, 0.0).astype(BF16)
    parts = jnp.concatenate(split3(table), axis=0).astype(BF16)
    found = jnp.dot(parts, third_hot[...], preferred_element_type=F32)
    n = block_x * block_y
    found = found[:n] + found[n : 2 * n] + found[2 * n :]
    found = jnp.sum(jnp.where(plane_mask, found, 0.0), axis=0, keepdims=True)
    live = lax.broadcasted_iota(I32, (1, rows), 1) < count[...]
    weight = jnp.where(live, found, 0.0)
    weight_ref[...] = weight

    split = [split3(-weight * normal[k, 0]) for k in range(3)]
    force = stack_rows([split[k][i] for i in range(3) for k in range(3)], 16).astype(BF16)
    partial = lax.dot_general(
        force, element_hot[...], (((1,), (1,)), ((), ())), preferred_element_type=F32
    )
    half = group // 2
    for k in range(3):
        total = partial[k : k + 1] + partial[3 + k : 4 + k] + partial[6 + k : 7 + k]
        for h in range(2):
            at = LOADS_AT + 2 * k + h
            for j in range(message.shape[0]):
                message[j, at : at + 1] = total[:, h * half : (h + 1) * half]


def derive(density, v0, v1, v2, pressure):
    m0, m1, m2 = density * v0, density * v1, density * v2
    energy = pressure * (1.0 / 0.4) + 0.5 * density * (v0 * v0 + v1 * v1 + v2 * v2)
    sound = jnp.sqrt(ratio_heat * pressure / density)
    return m0, m1, m2, energy, sound


RHO, V0, V1, V2, PRS, FRAC, M0, M1, M2, ENE, SND = range(11)


def face(along, low, high):
    vl, vh = low[V0 + along], high[V0 + along]
    speed = jnp.maximum(jnp.abs(vl) + low[SND], jnp.abs(vh) + high[SND])
    half = 0.5 * jnp.minimum(low[FRAC], high[FRAC])
    out = []
    for i, name in enumerate((RHO, M0, M1, M2, ENE)):
        if name == RHO:
            both = low[M0 + along] + high[M0 + along]
        elif name == ENE:
            both = vl * (low[ENE] + low[PRS]) + vh * (high[ENE] + high[PRS])
        else:
            both = vl * low[name] + vh * high[name]
            if i == 1 + along:
                both = both + (low[PRS] + high[PRS])
        out.append(half * (both - speed * (high[name] - low[name])))
    return out


def step_kernel(
    density,
    velocity,
    pressure,
    code,
    normal,
    mass,
    removed,
    motion,
    far_ref,
    near_ref,
    message,
    weight_ref,
    third_hot,
    plane_hot,
    element_hot,
    state_out,
    motion_out,
    cells,
    source,
    state,
    own_motion,
    state_sem,
    motion_sem,
):
    block_x, block_y, block_z = density.shape
    group = mass.shape[1]
    share = motion_out.shape[2]
    cols = message.shape[0]
    odd = lax.rem(lax.axis_index("slab"), 2)
    col = lax.axis_index("col")
    half = group // 2
    pad = TILE

    keep = 1.0 - removed[...].astype(F32)
    new = []
    for k in range(3):
        at = LOADS_AT + 2 * k
        load = message[0, at : at + 2]
        for j in range(1, cols):
            load = load + message[j, at : at + 2]
        load = jnp.concatenate([load[0:1], load[1:2]], axis=1)
        new.append((motion[k] + struct_step * load / mass[...]) * keep)
        own = new[k][:, 0:share]
        for j in range(1, cols):
            own = jnp.where(col == j, new[k][:, j * share : (j + 1) * share], own)
        own_motion[k] = own
    motion_copy = pltpu.make_async_copy(own_motion, motion_out, motion_sem)
    motion_copy.start()
    split = [split3(value) for value in new]
    stacked = stack_rows([split[k][i] for i in range(3) for k in range(3)], 16).astype(BF16)
    moved = jnp.dot(stacked, element_hot[...], preferred_element_type=F32)
    weight = weight_ref[...]
    work = jnp.zeros_like(weight)
    values = []
    for k in range(3):
        row = moved[k : k + 1] + moved[3 + k : 4 + k] + moved[6 + k : 7 + k]
        work = work + normal[k, 0] * row
        values.append(weight * normal[k, 0])
    values.append(weight * work)
    hot = plane_hot[...]
    parts = [split3(value) for value in values]
    for k in range(4):
        left = jnp.concatenate([hot * parts[k][i].astype(BF16) for i in range(3)], axis=0)
        found = lax.dot_general(
            left, third_hot[...], (((1,), (1,)), ((), ())), preferred_element_type=F32
        )
        n = block_x * block_y
        source[k] = (found[:n] + found[n : 2 * n] + found[2 * n :]).reshape(
            block_x, block_y, block_z
        )

    def store(plane, at, count, prims, fraction):
        full = list(prims) + [fraction] + list(derive(*prims))
        for name, value in enumerate(full):
            cells[name, plane, at : at + count] = value

    for x in range(block_x):
        for t in range(block_y // TILE):
            at = slice(t * TILE, (t + 1) * TILE)
            prims = [density[x, at]] + [velocity[k, x, at] for k in range(3)] + [pressure[x, at]]
            store(1 + x, pad + t * TILE, TILE, prims, code[x, at].astype(F32) * (1.0 / 16.0))
    for ref, plane in ((near_ref, 3 * (1 - odd)), (far_ref, 3 * odd)):
        for t in range(block_y // TILE):
            at = slice(t * TILE, (t + 1) * TILE)
            fraction = ref[5, at]
            live = fraction > 0.0
            prims = [jnp.where(live, ref[0, at], 1.0)] + [ref[1 + k, at] for k in range(3)]
            prims.append(jnp.where(live, ref[4, at], 1.0))
            store(plane, pad + t * TILE, TILE, prims, fraction)
    for other, inside, at in (
        (jnp.maximum(col - 1, 0), col > 0, pad - 1),
        (jnp.minimum(col + 1, cols - 1), col < cols - 1, pad + block_y),
    ):
        for x in range(block_x):
            prims = [message[other, f * block_x + x][None] for f in range(5)]
            fraction = message[other, 5 * block_x + x][None]
            store(1 + x, at, 1, prims, jnp.where(inside, fraction, 0.0))

    lane = lax.broadcasted_iota(I32, (TILE, block_z), 1)
    row = lax.broadcasted_iota(I32, (TILE, block_z), 0)

    def load(plane, at, along):
        out = {}
        for name in (RHO, V0 + along, PRS, FRAC, M0, M1, M2, ENE, SND):
            out[name] = cells[name, plane, at : at + TILE]
        return out

    for x in range(block_x):
        before = None
        for t in range(-1, block_y // TILE):
            at = pad + t * TILE
            upper = face(1, load(1 + x, at, 1), load(1 + x, at + 1, 1))
            turned = [pltpu.roll(value, 1, 0) for value in upper]
            if t < 0:
                before = turned
                continue
            total = [
                value - jnp.where(row == 0, old, fresh)
                for value, old, fresh in zip(upper, before, turned)
            ]
            before = turned
            own = load(1 + x, at, 2)
            right = {name: pltpu.roll(value, block_z - 1, 1) for name, value in own.items()}
            right[FRAC] = jnp.where(lane == block_z - 1, 0.0, right[FRAC])
            upper = face(2, own, right)
            total = [
                value + (flux - pltpu.roll(flux, 1, 1)) for value, flux in zip(total, upper)
            ]
            own = load(1 + x, at, 0)
            upper = face(0, own, load(2 + x, at, 0))
            lower = face(0, load(x, at, 0), own)
            total = [value + (u - v) for value, u, v in zip(total, upper, lower)]
            scale = step_ratio / own[FRAC]
            rows = slice(t * TILE, (t + 1) * TILE)
            for i, name in enumerate((RHO, M0, M1, M2, ENE)):
                change = total[i] - source[i - 1, x, rows] if i else total[i]
                state[i, x, rows] = own[name] - scale * change
        pltpu.make_async_copy(state.at[:, x], state_out.at[:, x], state_sem.at[x]).start()
    for x in range(block_x):
        pltpu.make_async_copy(state.at[:, x], state_out.at[:, x], state_sem.at[x]).wait()
    motion_copy.wait()


def in_vmem(*arrays):
    return [pltpu.with_memory_space_constraint(array, pltpu.VMEM) for array in arrays]


def local(
    density,
    velocity,
    pressure,
    fraction_code,
    interface_cell,
    interface_element,
    interface_count,
    wall_normal,
    element_mass,
    element_removed,
    element_velocity,
):
    block_x, block_y, block_z = density.shape
    rows = interface_cell.shape[2]
    group = element_mass.shape[1]
    slabs, cols = lax.axis_size("slab"), lax.axis_size("col")
    share = group // cols
    vmem = pl.BlockSpec(memory_space=pltpu.VMEM)
    hbm = pl.BlockSpec(memory_space=pltpu.HBM)
    given = (
        density,
        velocity,
        pressure,
        fraction_code,
        wall_normal,
        element_mass,
        element_removed,
        element_velocity,
    )
    results = pl.pallas_call(
        gather_kernel,
        out_shape=tuple(pltpu.VMEM(array.shape, array.dtype) for array in given)
        + (
            pltpu.VMEM((6, block_y, block_z), F32),
            pltpu.VMEM((6, block_y, block_z), F32),
            pltpu.VMEM((cols, 24, block_z), F32),
            pltpu.VMEM((1, rows), F32),
            pltpu.VMEM((block_z, rows), BF16),
            pltpu.VMEM((block_x * block_y, rows), BF16),
            pltpu.VMEM((group, rows), BF16),
        ),
        in_specs=[pl.BlockSpec(memory_space=pl.ANY)] + [hbm] * 10,
        out_specs=[vmem] * 15,
        scratch_shapes=[
            pltpu.VMEM(interface_count.shape, I32),
            pltpu.VMEM(interface_cell.shape, I32),
            pltpu.VMEM(interface_element.shape, I32),
            pltpu.SemaphoreType.DMA((11,)),
        ],
        name="gather_rows",
    )(
        interface_count,
        interface_cell,
        interface_element,
        *given,
    )
    kept, (far, near, message), hots = results[:8], results[8:11], results[11:]

    inner = [(i, i ^ 1) for i in range(slabs)]
    outer = [(i, i + 1 if i % 2 else i - 1) for i in range(1, slabs - 1)]
    far_in = lax.ppermute(far, "slab", outer)
    near_in = lax.ppermute(near, "slab", inner)
    message_in = lax.all_to_all(message, "col", 0, 0)

    state, new_motion = pl.pallas_call(
        step_kernel,
        out_shape=(
            jax.ShapeDtypeStruct((5, block_x, block_y, block_z), F32),
            jax.ShapeDtypeStruct((3, 1, share), F32),
        ),
        in_specs=[vmem] * 15,
        out_specs=[hbm, hbm],
        scratch_shapes=[
            pltpu.VMEM((11, block_x + 2, block_y + 2 * TILE, block_z), F32),
            pltpu.VMEM((4, block_x, block_y, block_z), F32),
            pltpu.VMEM((5, block_x, block_y, block_z), F32),
            pltpu.VMEM((3, 1, share), F32),
            pltpu.SemaphoreType.DMA((block_x,)),
            pltpu.SemaphoreType.DMA,
        ],
        name="step_cells",
    )(*in_vmem(*kept, far_in, near_in, message_in, *hots))
    return (state, new_motion)


def solution(mesh):
    placed = (
        P("slab", "col", None),
        P(None, "slab", "col", None),
        P("slab", "col", None),
        P("slab", "col", None),
        P("slab", "col", None),
        P("slab", "col", None),
        P("slab", "col"),
        P(None, "slab", "col", None),
        P("slab", None),
        P("slab", None),
        P(None, "slab", None),
    )
    return jax.shard_map(
        local,
        mesh=mesh,
        in_specs=placed,
        out_specs=(P(None, "slab", "col", None), P(None, "slab", "col")),
        check_vma=False,
    )
```

```python
import jax
import jax.numpy as jnp
from jax import lax
from jax.experimental import pallas as pl
from jax.experimental.pallas import tpu as pltpu
from jax.sharding import PartitionSpec as P

ratio_heat = 1.4
step_ratio = 0.1
struct_step = 1.0

F32, BF16, I32 = jnp.float32, jnp.bfloat16, jnp.int32
TILE = 8
LOADS_AT = 16


def split3(value):
    high = value.astype(BF16).astype(F32)
    rest = value - high
    middle = rest.astype(BF16).astype(F32)
    return high, middle, rest - middle


def stack_rows(rows, total):
    index = lax.broadcasted_iota(I32, (total, rows[0].shape[1]), 0)
    out = jnp.zeros((total, rows[0].shape[1]), F32)
    for at, row in enumerate(rows):
        out = jnp.where(index == at, row, out)
    return out


def gather_kernel(count_in, cell_in, element_in, *refs):
    given, kept = refs[:8], refs[8:16]
    message, weight_ref, third_hot, plane_hot, element_hot = refs[16:21]
    count, cell, element, sems = refs[21:]
    density, velocity, pressure, code, normal = kept[:5]
    pairs = [(cell_in, cell), (element_in, element), (count_in, count)] + list(zip(given, kept))
    copies = [pltpu.make_async_copy(a, b, sems.at[i]) for i, (a, b) in enumerate(pairs)]
    for copy in copies:
        copy.start()
    for copy in copies:
        copy.wait()
    block_x, block_y, block_z = density.shape
    rows = cell.shape[2]
    group = element_hot.shape[0]
    col = lax.axis_index("col")

    def edge(x, y):
        out = [density[x, y : y + 1]]
        out += [velocity[k, x, y : y + 1] for k in range(3)]
        out += [pressure[x, y : y + 1], code[x, y : y + 1].astype(F32) * (1.0 / 16.0)]
        return out

    for x in range(block_x):
        first, last = edge(x, 0), edge(x, block_y - 1)
        for j in range(message.shape[0]):
            for f in range(6):
                at = f * block_x + x
                message[j, at : at + 1] = jnp.where(col < j, last[f], first[f])

    fraction = code[...].astype(F32) * (1.0 / 16.0)
    table = (pressure[...] * (1.0 - fraction)).reshape(block_x * block_y, block_z)
    place = cell[0]
    third = jnp.bitwise_and(place, block_z - 1)
    plane = lax.shift_right_logical(place, block_z.bit_length() - 1)
    third_mask = lax.broadcasted_iota(I32, (block_z, rows), 0) == third
    third_hot[...] = jnp.where(third_mask, 1.0, 0.0).astype(BF16)
    plane_mask = lax.broadcasted_iota(I32, (block_x * block_y, rows), 0) == plane
    plane_hot[...] = jnp.where(plane_mask, 1.0, 0.0).astype(BF16)
    element_mask = lax.broadcasted_iota(I32, (group, rows), 0) == element[0]
    element_hot[...] = jnp.where(element_mask, 1.0, 0.0).astype(BF16)
    parts = jnp.concatenate(split3(table), axis=0).astype(BF16)
    found = jnp.dot(parts, third_hot[...], preferred_element_type=F32)
    n = block_x * block_y
    found = found[:n] + found[n : 2 * n] + found[2 * n :]
    found = jnp.sum(jnp.where(plane_mask, found, 0.0), axis=0, keepdims=True)
    live = lax.broadcasted_iota(I32, (1, rows), 1) < count[...]
    weight = jnp.where(live, found, 0.0)
    weight_ref[...] = weight

    split = [split3(-weight * normal[k, 0]) for k in range(3)]
    force = stack_rows([split[k][i] for i in range(3) for k in range(3)], 16).astype(BF16)
    partial = lax.dot_general(
        force, element_hot[...], (((1,), (1,)), ((), ())), preferred_element_type=F32
    )
    half = group // 2
    for k in range(3):
        total = partial[k : k + 1] + partial[3 + k : 4 + k] + partial[6 + k : 7 + k]
        for h in range(2):
            at = LOADS_AT + 2 * k + h
            for j in range(message.shape[0]):
                message[j, at : at + 1] = total[:, h * half : (h + 1) * half]


def derive(density, v0, v1, v2, pressure):
    m0, m1, m2 = density * v0, density * v1, density * v2
    energy = pressure * (1.0 / 0.4) + 0.5 * density * (v0 * v0 + v1 * v1 + v2 * v2)
    sound = jnp.sqrt(ratio_heat * pressure / density)
    return m0, m1, m2, energy, sound


RHO, V0, V1, V2, PRS, FRAC, M0, M1, M2, ENE, SND = range(11)


def face(along, low, high):
    vl, vh = low[V0 + along], high[V0 + along]
    speed = jnp.maximum(jnp.abs(vl) + low[SND], jnp.abs(vh) + high[SND])
    half = 0.5 * jnp.minimum(low[FRAC], high[FRAC])
    out = []
    for i, name in enumerate((RHO, M0, M1, M2, ENE)):
        if name == RHO:
            both = low[M0 + along] + high[M0 + along]
        elif name == ENE:
            both = vl * (low[ENE] + low[PRS]) + vh * (high[ENE] + high[PRS])
        else:
            both = vl * low[name] + vh * high[name]
            if i == 1 + along:
                both = both + (low[PRS] + high[PRS])
        out.append(half * (both - speed * (high[name] - low[name])))
    return out


def plane_kernel(density, velocity, pressure, code, far_ref, near_ref):
    odd = lax.rem(lax.axis_index("slab"), 2)
    for target, at in ((far_ref, odd), (near_ref, 1 - odd)):
        target[0] = density[at]
        for k in range(3):
            target[1 + k] = velocity[k, at]
        target[4] = pressure[at]
        target[5] = code[at].astype(F32) * (1.0 / 16.0)


def inner_kernel(density, velocity, pressure, code, total, terms):
    block_x, block_y, block_z = density.shape
    lane = lax.broadcasted_iota(I32, (TILE, block_z), 1)
    row = lax.broadcasted_iota(I32, (TILE, block_z), 0)
    tiles = block_y // TILE

    def prims(x, t):
        at = slice(t * TILE, (t + 1) * TILE)
        out = [density[x, at]] + [velocity[k, x, at] for k in range(3)]
        return out + [pressure[x, at], code[x, at].astype(F32) * (1.0 / 16.0)]

    def shifted(value, after):
        return jnp.where(row == TILE - 1, pltpu.roll(after, TILE - 1, 0), pltpu.roll(value, TILE - 1, 0))

    def full(x, t):
        own = prims(x, t)
        return dict(enumerate(own + list(derive(*own[:5]))))

    def keep(x, t, own):
        at = slice(t * TILE, (t + 1) * TILE)
        for i, name in enumerate((M0, M1, M2, ENE, SND)):
            terms[i, x, at] = own[name]

    for t in range(tiles):
        low, high = full(0, t), full(1, t)
        keep(0, t, low)
        keep(1, t, high)
        across = face(0, low, high)
        at = slice(t * TILE, (t + 1) * TILE)
        for x, own in ((0, low), (1, high)):
            right = {name: pltpu.roll(value, block_z - 1, 1) for name, value in own.items()}
            right[FRAC] = jnp.where(lane == block_z - 1, 0.0, right[FRAC])
            upper = face(2, own, right)
            for i in range(5):
                value = upper[i] - pltpu.roll(upper[i], 1, 1)
                total[i, x, at] = value + across[i] if x == 0 else value - across[i]
    for x in range(block_x):
        before = None
        for t in range(tiles):
            at = slice(t * TILE, (t + 1) * TILE)

            def load(u):
                at = slice(u * TILE, (u + 1) * TILE)
                out = {RHO: density[x, at], V1: velocity[1, x, at], PRS: pressure[x, at]}
                out[FRAC] = code[x, at].astype(F32) * (1.0 / 16.0)
                for i, name in enumerate((M0, M1, M2, ENE, SND)):
                    out[name] = terms[i, x, at]
                return out

            own = load(t)
            after = load(min(t + 1, tiles - 1))
            above = {name: shifted(own[name], after[name]) for name in own}
            if t == tiles - 1:
                above[FRAC] = jnp.where(row == TILE - 1, 0.0, above[FRAC])
            upper = face(1, own, above)
            turned = [pltpu.roll(value, 1, 0) for value in upper]
            for i in range(5):
                first = jnp.zeros_like(turned[i]) if before is None else before[i]
                total[i, x, at] += upper[i] - jnp.where(row == 0, first, turned[i])
            before = turned


def step_kernel(
    density,
    velocity,
    pressure,
    code,
    normal,
    mass,
    removed,
    motion,
    total,
    terms,
    far_ref,
    near_ref,
    message,
    weight_ref,
    third_hot,
    plane_hot,
    element_hot,
    state_out,
    motion_out,
    source,
    state,
    own_motion,
    state_sem,
    motion_sem,
):
    block_x, block_y, block_z = density.shape
    group = mass.shape[1]
    share = motion_out.shape[2]
    cols = message.shape[0]
    odd = lax.rem(lax.axis_index("slab"), 2)
    col = lax.axis_index("col")
    tiles = block_y // TILE

    keep = 1.0 - removed[...].astype(F32)
    new = []
    for k in range(3):
        at = LOADS_AT + 2 * k
        load = message[0, at : at + 2]
        for j in range(1, cols):
            load = load + message[j, at : at + 2]
        load = jnp.concatenate([load[0:1], load[1:2]], axis=1)
        new.append((motion[k] + struct_step * load / mass[...]) * keep)
        own = new[k][:, 0:share]
        for j in range(1, cols):
            own = jnp.where(col == j, new[k][:, j * share : (j + 1) * share], own)
        own_motion[k] = own
    motion_copy = pltpu.make_async_copy(own_motion, motion_out, motion_sem)
    motion_copy.start()
    split = [split3(value) for value in new]
    stacked = stack_rows([split[k][i] for i in range(3) for k in range(3)], 16).astype(BF16)
    moved = jnp.dot(stacked, element_hot[...], preferred_element_type=F32)
    weight = weight_ref[...]
    work = jnp.zeros_like(weight)
    values = []
    for k in range(3):
        row = moved[k : k + 1] + moved[3 + k : 4 + k] + moved[6 + k : 7 + k]
        work = work + normal[k, 0] * row
        values.append(weight * normal[k, 0])
    values.append(weight * work)
    hot = plane_hot[...]
    parts = [split3(value) for value in values]
    for k in range(4):
        left = jnp.concatenate([hot * parts[k][i].astype(BF16) for i in range(3)], axis=0)
        found = lax.dot_general(
            left, third_hot[...], (((1,), (1,)), ((), ())), preferred_element_type=F32
        )
        n = block_x * block_y
        source[k] = (found[:n] + found[n : 2 * n] + found[2 * n :]).reshape(
            block_x, block_y, block_z
        )

    def other(prims, fraction):
        live = fraction > 0.0
        prims = [jnp.where(live, prims[0], 1.0)] + prims[1:4] + [jnp.where(live, prims[4], 1.0)]
        return dict(enumerate(prims + [fraction] + list(derive(*prims))))

    def edge(along_y):
        out = {RHO: density[:, along_y], PRS: pressure[:, along_y]}
        for k in range(3):
            out[V0 + k] = velocity[k, :, along_y]
            out[M0 + k] = terms[k, :, along_y]
        out[FRAC] = code[:, along_y].astype(F32) * (1.0 / 16.0)
        out[ENE], out[SND] = terms[3, :, along_y], terms[4, :, along_y]
        return out

    def arrived(j, inside):
        rows = [message[j, f * block_x : (f + 1) * block_x] for f in range(6)]
        return other(rows[:5], jnp.where(inside, rows[5], 0.0))

    bottom = face(1, arrived(jnp.maximum(col - 1, 0), col > 0), edge(0))
    top = face(1, edge(block_y - 1), arrived(jnp.minimum(col + 1, cols - 1), col < cols - 1))

    row = lax.broadcasted_iota(I32, (TILE, block_z), 0)
    for x in range(block_x):
        for t in range(tiles):
            at = slice(t * TILE, (t + 1) * TILE)
            near = [near_ref[f, at] for f in range(6)]
            far = [far_ref[f, at] for f in range(6)]
            use_near = odd == (1 - x)
            got = [jnp.where(use_near, a, b) for a, b in zip(near, far)]
            beyond = other(got[:5], got[5])
            own = {RHO: density[x, at], PRS: pressure[x, at], V0: velocity[0, x, at]}
            for k in range(3):
                own[M0 + k] = terms[k, x, at]
            own[FRAC] = code[x, at].astype(F32) * (1.0 / 16.0)
            own[ENE], own[SND] = terms[3, x, at], terms[4, x, at]
            flux = face(0, beyond, own) if x == 0 else face(0, own, beyond)
            scale = step_ratio / own[FRAC]
            for i, name in enumerate((RHO, M0, M1, M2, ENE)):
                change = total[i, x, at] - flux[i] if x == 0 else total[i, x, at] + flux[i]
                if t == 0:
                    change = change - jnp.where(row == 0, bottom[i][x : x + 1], 0.0)
                if t == tiles - 1:
                    change = change + jnp.where(row == TILE - 1, top[i][x : x + 1], 0.0)
                if i:
                    change = change - source[i - 1, x, at]
                state[i, x, at] = own[name] - scale * change
        pltpu.make_async_copy(state.at[:, x], state_out.at[:, x], state_sem.at[x]).start()
    for x in range(block_x):
        pltpu.make_async_copy(state.at[:, x], state_out.at[:, x], state_sem.at[x]).wait()
    motion_copy.wait()


def in_vmem(*arrays):
    return [pltpu.with_memory_space_constraint(array, pltpu.VMEM) for array in arrays]


def local(
    density,
    velocity,
    pressure,
    fraction_code,
    interface_cell,
    interface_element,
    interface_count,
    wall_normal,
    element_mass,
    element_removed,
    element_velocity,
):
    block_x, block_y, block_z = density.shape
    rows = interface_cell.shape[2]
    group = element_mass.shape[1]
    slabs, cols = lax.axis_size("slab"), lax.axis_size("col")
    share = group // cols
    vmem = pl.BlockSpec(memory_space=pltpu.VMEM)
    hbm = pl.BlockSpec(memory_space=pltpu.HBM)
    given = (
        density,
        velocity,
        pressure,
        fraction_code,
        wall_normal,
        element_mass,
        element_removed,
        element_velocity,
    )
    results = pl.pallas_call(
        gather_kernel,
        out_shape=tuple(pltpu.VMEM(array.shape, array.dtype) for array in given)
        + (
            pltpu.VMEM((cols, 24, block_z), F32),
            pltpu.VMEM((1, rows), F32),
            pltpu.VMEM((block_z, rows), BF16),
            pltpu.VMEM((block_x * block_y, rows), BF16),
            pltpu.VMEM((group, rows), BF16),
        ),
        in_specs=[pl.BlockSpec(memory_space=pl.ANY)] + [hbm] * 10,
        out_specs=[vmem] * 13,
        scratch_shapes=[
            pltpu.VMEM(interface_count.shape, I32),
            pltpu.VMEM(interface_cell.shape, I32),
            pltpu.VMEM(interface_element.shape, I32),
            pltpu.SemaphoreType.DMA((11,)),
        ],
        name="gather_rows",
    )(
        interface_count,
        interface_cell,
        interface_element,
        *given,
    )
    kept, message, hots = results[:8], results[8], results[9:]

    message_in = lax.all_to_all(message, "col", 0, 0)
    planes = pltpu.VMEM((6, block_y, block_z), F32)
    far, near = pl.pallas_call(
        plane_kernel,
        out_shape=(planes, planes),
        in_specs=[vmem] * 4,
        out_specs=[vmem] * 2,
        cost_estimate=pl.CostEstimate(flops=100000, bytes_accessed=100000, transcendentals=0),
        name="pack_planes",
    )(*in_vmem(*kept[:4]))
    total, terms = pl.pallas_call(
        inner_kernel,
        out_shape=(
            pltpu.VMEM((5, block_x, block_y, block_z), F32),
            pltpu.VMEM((5, block_x, block_y, block_z), F32),
        ),
        in_specs=[vmem] * 4,
        out_specs=[vmem] * 2,
        cost_estimate=pl.CostEstimate(flops=10000000000, bytes_accessed=100000000, transcendentals=0),
        name="inner_faces",
    )(*in_vmem(*kept[:4]))
    inner = [(i, i ^ 1) for i in range(slabs)]
    outer = [(i, i + 1 if i % 2 else i - 1) for i in range(1, slabs - 1)]
    far_in = lax.ppermute(far, "slab", outer)
    near_in = lax.ppermute(near, "slab", inner)

    state, new_motion = pl.pallas_call(
        step_kernel,
        out_shape=(
            jax.ShapeDtypeStruct((5, block_x, block_y, block_z), F32),
            jax.ShapeDtypeStruct((3, 1, share), F32),
        ),
        in_specs=[vmem] * 17,
        out_specs=[hbm, hbm],
        scratch_shapes=[
            pltpu.VMEM((4, block_x, block_y, block_z), F32),
            pltpu.VMEM((5, block_x, block_y, block_z), F32),
            pltpu.VMEM((3, 1, share), F32),
            pltpu.SemaphoreType.DMA((block_x,)),
            pltpu.SemaphoreType.DMA,
        ],
        name="step_cells",
    )(*in_vmem(*kept, total, terms, far_in, near_in, message_in, *hots))
    return (state, new_motion)


def solution(mesh):
    placed = (
        P("slab", "col", None),
        P(None, "slab", "col", None),
        P("slab", "col", None),
        P("slab", "col", None),
        P("slab", "col", None),
        P("slab", "col", None),
        P("slab", "col"),
        P(None, "slab", "col", None),
        P("slab", None),
        P("slab", None),
        P(None, "slab", None),
    )
    return jax.shard_map(
        local,
        mesh=mesh,
        in_specs=placed,
        out_specs=(P(None, "slab", "col", None), P(None, "slab", "col")),
        check_vma=False,
    )
```

```python
import jax
import jax.numpy as jnp
from jax import lax
from jax.experimental import pallas as pl
from jax.experimental.pallas import tpu as pltpu
from jax.sharding import PartitionSpec as P

ratio_heat = 1.4
step_ratio = 0.1
struct_step = 1.0

F32, BF16, I32 = jnp.float32, jnp.bfloat16, jnp.int32
TILE = 8
LOADS_AT = 16


def split3(value):
    high = value.astype(BF16).astype(F32)
    rest = value - high
    middle = rest.astype(BF16).astype(F32)
    return high, middle, rest - middle


def stack_rows(rows, total):
    index = lax.broadcasted_iota(I32, (total, rows[0].shape[1]), 0)
    out = jnp.zeros((total, rows[0].shape[1]), F32)
    for at, row in enumerate(rows):
        out = jnp.where(index == at, row, out)
    return out


def gather_kernel(count_in, cell_in, element_in, *refs):
    given, kept = refs[:8], refs[8:16]
    message, weight_ref, third_hot, plane_hot, element_hot = refs[16:21]
    count, cell, element, sems = refs[21:]
    density, velocity, pressure, code, normal = kept[:5]
    pairs = [(cell_in, cell), (element_in, element), (count_in, count)]
    pairs += [(given[i], kept[i]) for i in (2, 3, 4, 0, 1, 5, 6, 7)]
    copies = [pltpu.make_async_copy(a, b, sems.at[i]) for i, (a, b) in enumerate(pairs)]
    for copy in copies:
        copy.start()
    block_x, block_y, block_z = density.shape
    rows = cell.shape[2]
    group = element_hot.shape[0]
    col = lax.axis_index("col")

    copies[0].wait()
    copies[1].wait()
    place = cell[0]
    third = jnp.bitwise_and(place, block_z - 1)
    plane = lax.shift_right_logical(place, block_z.bit_length() - 1)
    third_mask = lax.broadcasted_iota(I32, (block_z, rows), 0) == third
    third_hot[...] = jnp.where(third_mask, 1.0, 0.0).astype(BF16)
    plane_mask = lax.broadcasted_iota(I32, (block_x * block_y, rows), 0) == plane
    plane_hot[...] = jnp.where(plane_mask, 1.0, 0.0).astype(BF16)
    element_mask = lax.broadcasted_iota(I32, (group, rows), 0) == element[0]
    element_hot[...] = jnp.where(element_mask, 1.0, 0.0).astype(BF16)
    for copy in copies[2:6]:
        copy.wait()
    fraction = code[...].astype(F32) * (1.0 / 16.0)
    table = (pressure[...] * (1.0 - fraction)).reshape(block_x * block_y, block_z)
    parts = jnp.concatenate(split3(table), axis=0).astype(BF16)
    found = jnp.dot(parts, third_hot[...], preferred_element_type=F32)
    n = block_x * block_y
    found = found[:n] + found[n : 2 * n] + found[2 * n :]
    found = jnp.sum(jnp.where(plane_mask, found, 0.0), axis=0, keepdims=True)
    live = lax.broadcasted_iota(I32, (1, rows), 1) < count[...]
    weight = jnp.where(live, found, 0.0)
    weight_ref[...] = weight

    for copy in copies[6:]:
        copy.wait()
    def edge(x, y):
        out = [density[x, y : y + 1]]
        out += [velocity[k, x, y : y + 1] for k in range(3)]
        out += [pressure[x, y : y + 1], code[x, y : y + 1].astype(F32) * (1.0 / 16.0)]
        return out

    for x in range(block_x):
        first, last = edge(x, 0), edge(x, block_y - 1)
        for j in range(message.shape[0]):
            for f in range(6):
                at = f * block_x + x
                message[j, at : at + 1] = jnp.where(col < j, last[f], first[f])

    split = [split3(-weight * normal[k, 0]) for k in range(3)]
    force = stack_rows([split[k][i] for i in range(3) for k in range(3)], 16).astype(BF16)
    partial = lax.dot_general(
        force, element_hot[...], (((1,), (1,)), ((), ())), preferred_element_type=F32
    )
    half = group // 2
    for k in range(3):
        total = partial[k : k + 1] + partial[3 + k : 4 + k] + partial[6 + k : 7 + k]
        for h in range(2):
            at = LOADS_AT + 2 * k + h
            for j in range(message.shape[0]):
                message[j, at : at + 1] = total[:, h * half : (h + 1) * half]


def derive(density, v0, v1, v2, pressure):
    m0, m1, m2 = density * v0, density * v1, density * v2
    energy = pressure * (1.0 / 0.4) + 0.5 * density * (v0 * v0 + v1 * v1 + v2 * v2)
    sound = jnp.sqrt(ratio_heat * pressure / density)
    return m0, m1, m2, energy, sound


RHO, V0, V1, V2, PRS, FRAC, M0, M1, M2, ENE, SND = range(11)


def face(along, low, high):
    vl, vh = low[V0 + along], high[V0 + along]
    speed = jnp.maximum(jnp.abs(vl) + low[SND], jnp.abs(vh) + high[SND])
    half = 0.5 * jnp.minimum(low[FRAC], high[FRAC])
    out = []
    for i, name in enumerate((RHO, M0, M1, M2, ENE)):
        if name == RHO:
            both = low[M0 + along] + high[M0 + along]
        elif name == ENE:
            both = vl * (low[ENE] + low[PRS]) + vh * (high[ENE] + high[PRS])
        else:
            both = vl * low[name] + vh * high[name]
            if i == 1 + along:
                both = both + (low[PRS] + high[PRS])
        out.append(half * (both - speed * (high[name] - low[name])))
    return out


def plane_kernel(density, velocity, pressure, code, far_ref, near_ref):
    odd = lax.rem(lax.axis_index("slab"), 2)
    for target, at in ((far_ref, odd), (near_ref, 1 - odd)):
        target[0] = density[at]
        for k in range(3):
            target[1 + k] = velocity[k, at]
        target[4] = pressure[at]
        target[5] = code[at].astype(F32) * (1.0 / 16.0)


def scatter(hot, third_hot, row):
    left = jnp.concatenate([hot * part.astype(BF16) for part in split3(row)], axis=0)
    found = lax.dot_general(
        left, third_hot[...], (((1,), (1,)), ((), ())), preferred_element_type=F32
    )
    n = hot.shape[0]
    return found[:n] + found[n : 2 * n] + found[2 * n :]


def inner_kernel(
    density, velocity, pressure, code, normal, weight, third_hot, plane_hot, source, total, terms
):
    hot = plane_hot[...]
    for k in range(3):
        source[k] = scatter(hot, third_hot, weight[...] * normal[k, 0]).reshape(density.shape)
    block_x, block_y, block_z = density.shape
    lane = lax.broadcasted_iota(I32, (TILE, block_z), 1)
    row = lax.broadcasted_iota(I32, (TILE, block_z), 0)
    tiles = block_y // TILE

    def prims(x, t):
        at = slice(t * TILE, (t + 1) * TILE)
        out = [density[x, at]] + [velocity[k, x, at] for k in range(3)]
        return out + [pressure[x, at], code[x, at].astype(F32) * (1.0 / 16.0)]

    def shifted(value, after):
        return jnp.where(row == TILE - 1, pltpu.roll(after, TILE - 1, 0), pltpu.roll(value, TILE - 1, 0))

    def full(x, t):
        own = prims(x, t)
        return dict(enumerate(own + list(derive(*own[:5]))))

    def keep(x, t, own):
        at = slice(t * TILE, (t + 1) * TILE)
        for i, name in enumerate((M0, M1, M2, ENE, SND)):
            terms[i, x, at] = own[name]

    for t in range(tiles):
        low, high = full(0, t), full(1, t)
        keep(0, t, low)
        keep(1, t, high)
        across = face(0, low, high)
        at = slice(t * TILE, (t + 1) * TILE)
        for x, own in ((0, low), (1, high)):
            right = {name: pltpu.roll(value, block_z - 1, 1) for name, value in own.items()}
            right[FRAC] = jnp.where(lane == block_z - 1, 0.0, right[FRAC])
            upper = face(2, own, right)
            for i in range(5):
                value = upper[i] - pltpu.roll(upper[i], 1, 1)
                total[i, x, at] = value + across[i] if x == 0 else value - across[i]
    for x in range(block_x):
        before = None
        for t in range(tiles):
            at = slice(t * TILE, (t + 1) * TILE)

            def load(u):
                at = slice(u * TILE, (u + 1) * TILE)
                out = {RHO: density[x, at], V1: velocity[1, x, at], PRS: pressure[x, at]}
                out[FRAC] = code[x, at].astype(F32) * (1.0 / 16.0)
                for i, name in enumerate((M0, M1, M2, ENE, SND)):
                    out[name] = terms[i, x, at]
                return out

            own = load(t)
            after = load(min(t + 1, tiles - 1))
            above = {name: shifted(own[name], after[name]) for name in own}
            if t == tiles - 1:
                above[FRAC] = jnp.where(row == TILE - 1, 0.0, above[FRAC])
            upper = face(1, own, above)
            turned = [pltpu.roll(value, 1, 0) for value in upper]
            for i in range(5):
                first = jnp.zeros_like(turned[i]) if before is None else before[i]
                total[i, x, at] += upper[i] - jnp.where(row == 0, first, turned[i])
            before = turned


def step_kernel(
    density,
    velocity,
    pressure,
    code,
    normal,
    mass,
    removed,
    motion,
    pushed,
    total,
    terms,
    far_ref,
    near_ref,
    message,
    weight_ref,
    third_hot,
    plane_hot,
    element_hot,
    state_out,
    motion_out,
    source,
    state,
    own_motion,
    state_sem,
    motion_sem,
):
    block_x, block_y, block_z = density.shape
    group = mass.shape[1]
    share = motion_out.shape[2]
    cols = message.shape[0]
    odd = lax.rem(lax.axis_index("slab"), 2)
    col = lax.axis_index("col")
    tiles = block_y // TILE

    keep = 1.0 - removed[...].astype(F32)
    new = []
    for k in range(3):
        at = LOADS_AT + 2 * k
        load = message[0, at : at + 2]
        for j in range(1, cols):
            load = load + message[j, at : at + 2]
        load = jnp.concatenate([load[0:1], load[1:2]], axis=1)
        new.append((motion[k] + struct_step * load / mass[...]) * keep)
        own = new[k][:, 0:share]
        for j in range(1, cols):
            own = jnp.where(col == j, new[k][:, j * share : (j + 1) * share], own)
        own_motion[k] = own
    motion_copy = pltpu.make_async_copy(own_motion, motion_out, motion_sem)
    motion_copy.start()
    split = [split3(value) for value in new]
    stacked = stack_rows([split[k][i] for i in range(3) for k in range(3)], 16).astype(BF16)
    moved = jnp.dot(stacked, element_hot[...], preferred_element_type=F32)
    weight = weight_ref[...]
    work = jnp.zeros_like(weight)
    for k in range(3):
        row = moved[k : k + 1] + moved[3 + k : 4 + k] + moved[6 + k : 7 + k]
        work = work + normal[k, 0] * row
    source[...] = scatter(plane_hot[...], third_hot, weight * work).reshape(source.shape)

    def other(prims, fraction):
        live = fraction > 0.0
        prims = [jnp.where(live, prims[0], 1.0)] + prims[1:4] + [jnp.where(live, prims[4], 1.0)]
        return dict(enumerate(prims + [fraction] + list(derive(*prims))))

    def edge(along_y):
        out = {RHO: density[:, along_y], PRS: pressure[:, along_y]}
        for k in range(3):
            out[V0 + k] = velocity[k, :, along_y]
            out[M0 + k] = terms[k, :, along_y]
        out[FRAC] = code[:, along_y].astype(F32) * (1.0 / 16.0)
        out[ENE], out[SND] = terms[3, :, along_y], terms[4, :, along_y]
        return out

    def arrived(j, inside):
        rows = [message[j, f * block_x : (f + 1) * block_x] for f in range(6)]
        return other(rows[:5], jnp.where(inside, rows[5], 0.0))

    bottom = face(1, arrived(jnp.maximum(col - 1, 0), col > 0), edge(0))
    top = face(1, edge(block_y - 1), arrived(jnp.minimum(col + 1, cols - 1), col < cols - 1))

    row = lax.broadcasted_iota(I32, (TILE, block_z), 0)
    for x in range(block_x):
        for t in range(tiles):
            at = slice(t * TILE, (t + 1) * TILE)
            near = [near_ref[f, at] for f in range(6)]
            far = [far_ref[f, at] for f in range(6)]
            use_near = odd == (1 - x)
            got = [jnp.where(use_near, a, b) for a, b in zip(near, far)]
            beyond = other(got[:5], got[5])
            own = {RHO: density[x, at], PRS: pressure[x, at], V0: velocity[0, x, at]}
            for k in range(3):
                own[M0 + k] = terms[k, x, at]
            own[FRAC] = code[x, at].astype(F32) * (1.0 / 16.0)
            own[ENE], own[SND] = terms[3, x, at], terms[4, x, at]
            flux = face(0, beyond, own) if x == 0 else face(0, own, beyond)
            scale = step_ratio / own[FRAC]
            for i, name in enumerate((RHO, M0, M1, M2, ENE)):
                change = total[i, x, at] - flux[i] if x == 0 else total[i, x, at] + flux[i]
                if t == 0:
                    change = change - jnp.where(row == 0, bottom[i][x : x + 1], 0.0)
                if t == tiles - 1:
                    change = change + jnp.where(row == TILE - 1, top[i][x : x + 1], 0.0)
                if i:
                    change = change - (source[x, at] if i == 4 else pushed[i - 1, x, at])
                state[i, x, at] = own[name] - scale * change
        pltpu.make_async_copy(state.at[:, x], state_out.at[:, x], state_sem.at[x]).start()
    for x in range(block_x):
        pltpu.make_async_copy(state.at[:, x], state_out.at[:, x], state_sem.at[x]).wait()
    motion_copy.wait()


def in_vmem(*arrays):
    return [pltpu.with_memory_space_constraint(array, pltpu.VMEM) for array in arrays]


def local(
    density,
    velocity,
    pressure,
    fraction_code,
    interface_cell,
    interface_element,
    interface_count,
    wall_normal,
    element_mass,
    element_removed,
    element_velocity,
):
    block_x, block_y, block_z = density.shape
    rows = interface_cell.shape[2]
    group = element_mass.shape[1]
    slabs, cols = lax.axis_size("slab"), lax.axis_size("col")
    share = group // cols
    vmem = pl.BlockSpec(memory_space=pltpu.VMEM)
    hbm = pl.BlockSpec(memory_space=pltpu.HBM)
    given = (
        density,
        velocity,
        pressure,
        fraction_code,
        wall_normal,
        element_mass,
        element_removed,
        element_velocity,
    )
    results = pl.pallas_call(
        gather_kernel,
        out_shape=tuple(pltpu.VMEM(array.shape, array.dtype) for array in given)
        + (
            pltpu.VMEM((cols, 24, block_z), F32),
            pltpu.VMEM((1, rows), F32),
            pltpu.VMEM((block_z, rows), BF16),
            pltpu.VMEM((block_x * block_y, rows), BF16),
            pltpu.VMEM((group, rows), BF16),
        ),
        in_specs=[pl.BlockSpec(memory_space=pl.ANY)] + [hbm] * 10,
        out_specs=[vmem] * 13,
        scratch_shapes=[
            pltpu.VMEM(interface_count.shape, I32),
            pltpu.VMEM(interface_cell.shape, I32),
            pltpu.VMEM(interface_element.shape, I32),
            pltpu.SemaphoreType.DMA((11,)),
        ],
        name="gather_rows",
    )(
        interface_count,
        interface_cell,
        interface_element,
        *given,
    )
    kept, message, hots = results[:8], results[8], results[9:]

    message_in = lax.all_to_all(message, "col", 0, 0)
    planes = pltpu.VMEM((6, block_y, block_z), F32)
    far, near = pl.pallas_call(
        plane_kernel,
        out_shape=(planes, planes),
        in_specs=[vmem] * 4,
        out_specs=[vmem] * 2,
        cost_estimate=pl.CostEstimate(flops=100000, bytes_accessed=100000, transcendentals=0),
        name="pack_planes",
    )(*in_vmem(*kept[:4]))
    pushed, total, terms = pl.pallas_call(
        inner_kernel,
        out_shape=(
            pltpu.VMEM((3, block_x, block_y, block_z), F32),
            pltpu.VMEM((5, block_x, block_y, block_z), F32),
            pltpu.VMEM((5, block_x, block_y, block_z), F32),
        ),
        in_specs=[vmem] * 8,
        out_specs=[vmem] * 3,
        cost_estimate=pl.CostEstimate(flops=10000000000, bytes_accessed=100000000, transcendentals=0),
        name="inner_faces",
    )(*in_vmem(*kept[:5], *hots[:3]))
    inner = [(i, i ^ 1) for i in range(slabs)]
    outer = [(i, i + 1 if i % 2 else i - 1) for i in range(1, slabs - 1)]
    far_in = lax.ppermute(far, "slab", outer)
    near_in = lax.ppermute(near, "slab", inner)

    state, new_motion = pl.pallas_call(
        step_kernel,
        out_shape=(
            jax.ShapeDtypeStruct((5, block_x, block_y, block_z), F32),
            jax.ShapeDtypeStruct((3, 1, share), F32),
        ),
        in_specs=[vmem] * 18,
        out_specs=[hbm, hbm],
        scratch_shapes=[
            pltpu.VMEM((block_x, block_y, block_z), F32),
            pltpu.VMEM((5, block_x, block_y, block_z), F32),
            pltpu.VMEM((3, 1, share), F32),
            pltpu.SemaphoreType.DMA((block_x,)),
            pltpu.SemaphoreType.DMA,
        ],
        name="step_cells",
    )(*in_vmem(*kept, pushed, total, terms, far_in, near_in, message_in, *hots))
    return (state, new_motion)


def solution(mesh):
    placed = (
        P("slab", "col", None),
        P(None, "slab", "col", None),
        P("slab", "col", None),
        P("slab", "col", None),
        P("slab", "col", None),
        P("slab", "col", None),
        P("slab", "col"),
        P(None, "slab", "col", None),
        P("slab", None),
        P("slab", None),
        P(None, "slab", None),
    )
    return jax.shard_map(
        local,
        mesh=mesh,
        in_specs=placed,
        out_specs=(P(None, "slab", "col", None), P(None, "slab", "col")),
        check_vma=False,
    )
```

```python
import jax
import jax.numpy as jnp
from jax import lax
from jax.experimental import pallas as pl
from jax.experimental.pallas import tpu as pltpu
from jax.sharding import PartitionSpec as P

ratio_heat = 1.4
step_ratio = 0.1
struct_step = 1.0

F32, BF16, I32 = jnp.float32, jnp.bfloat16, jnp.int32
VMEM_BYTES = 8 * 2**20
TILE = 8
LANES = 128
LOADS_AT = 24
MESSAGE_ROWS = 40


def split3(value):
    high = value.astype(BF16).astype(F32)
    rest = value - high
    middle = rest.astype(BF16).astype(F32)
    return high, middle, rest - middle


def stack_rows(rows, total):
    index = lax.broadcasted_iota(I32, (total, rows[0].shape[1]), 0)
    out = jnp.zeros((total, rows[0].shape[1]), F32)
    for at, row in enumerate(rows):
        out = jnp.where(index == at, row, out)
    return out


def gather_kernel(count_in, cell_in, element_in, *refs):
    given, kept = refs[:8], refs[8:16]
    message_out, weight_ref, third_hot, plane_hot, element_hot = refs[16:21]
    count, cell, element, message, sems, sent = refs[21:]
    density, velocity, pressure, code, normal = kept[:5]
    pairs = [(cell_in, cell), (element_in, element), (count_in, count)]
    pairs += [(given[i], kept[i]) for i in (2, 3, 4, 0, 1, 5, 6, 7)]
    copies = [pltpu.make_async_copy(a, b, sems.at[i]) for i, (a, b) in enumerate(pairs)]
    for copy in copies:
        copy.start()
    block_x, block_y, block_z = density.shape
    rows = cell.shape[2]
    group = element_hot.shape[0]
    col = lax.axis_index("col")

    copies[0].wait()
    copies[1].wait()
    place = cell[0]
    third = jnp.bitwise_and(place, block_z - 1)
    plane = lax.shift_right_logical(place, block_z.bit_length() - 1)
    third_mask = lax.broadcasted_iota(I32, (block_z, rows), 0) == third
    third_hot[...] = jnp.where(third_mask, 1.0, 0.0).astype(BF16)
    plane_mask = lax.broadcasted_iota(I32, (block_x * block_y, rows), 0) == plane
    plane_hot[...] = jnp.where(plane_mask, 1.0, 0.0).astype(BF16)
    element_mask = lax.broadcasted_iota(I32, (group, rows), 0) == element[0]
    element_hot[...] = jnp.where(element_mask, 1.0, 0.0).astype(BF16)
    for copy in copies[2:6]:
        copy.wait()
    fraction = code[...].astype(F32) * (1.0 / 16.0)
    table = (pressure[...] * (1.0 - fraction)).reshape(block_x * block_y, block_z)
    parts = jnp.concatenate(split3(table), axis=0).astype(BF16)
    found = jnp.dot(parts, third_hot[...], preferred_element_type=F32)
    n = block_x * block_y
    found = found[:n] + found[n : 2 * n] + found[2 * n :]
    found = jnp.sum(jnp.where(plane_mask, found, 0.0), axis=0, keepdims=True)
    live = lax.broadcasted_iota(I32, (1, rows), 1) < count[...]
    weight = jnp.where(live, found, 0.0)
    weight_ref[...] = weight

    for copy in copies[6:]:
        copy.wait()
    def edge(x, y):
        out = [density[x, y : y + 1]]
        out += [velocity[k, x, y : y + 1] for k in range(3)]
        out += [pressure[x, y : y + 1], code[x, y : y + 1].astype(F32) * (1.0 / 16.0)]
        return out

    for x in range(block_x):
        first, last = edge(x, 0), edge(x, block_y - 1)
        for j in range(message.shape[0]):
            for f in range(6):
                row = jnp.where(col < j, last[f], first[f])
                for h in range(2):
                    at = (2 * f + h) * block_x + x
                    message[j, at : at + 1] = row[:, h * LANES : (h + 1) * LANES]
    for j in range(message.shape[0]):
        message[j, LOADS_AT + 12 :] = jnp.zeros((4, LANES), F32)
    edges = slice(0, LOADS_AT)
    edge_copy = pltpu.make_async_copy(message.at[:, edges], message_out.at[:, edges], sent.at[0])
    edge_copy.start()

    split = [split3(-weight * normal[k, 0]) for k in range(3)]
    force = stack_rows([split[k][i] for i in range(3) for k in range(3)], 16).astype(BF16)
    partial = lax.dot_general(
        force, element_hot[...], (((1,), (1,)), ((), ())), preferred_element_type=F32
    )
    quarters = group // LANES
    for k in range(3):
        total = partial[k : k + 1] + partial[3 + k : 4 + k] + partial[6 + k : 7 + k]
        for q in range(quarters):
            at = LOADS_AT + quarters * k + q
            for j in range(message.shape[0]):
                message[j, at : at + 1] = total[:, q * LANES : (q + 1) * LANES]
    loads = slice(LOADS_AT, MESSAGE_ROWS)
    load_copy = pltpu.make_async_copy(message.at[:, loads], message_out.at[:, loads], sent.at[1])
    load_copy.start()
    edge_copy.wait()
    load_copy.wait()


def derive(density, v0, v1, v2, pressure):
    m0, m1, m2 = density * v0, density * v1, density * v2
    energy = pressure * (1.0 / 0.4) + 0.5 * density * (v0 * v0 + v1 * v1 + v2 * v2)
    sound = jnp.sqrt(ratio_heat * pressure / density)
    return m0, m1, m2, energy, sound


RHO, V0, V1, V2, PRS, FRAC, M0, M1, M2, ENE, SND = range(11)


def face(along, low, high):
    vl, vh = low[V0 + along], high[V0 + along]
    speed = jnp.maximum(jnp.abs(vl) + low[SND], jnp.abs(vh) + high[SND])
    half = 0.5 * jnp.minimum(low[FRAC], high[FRAC])
    out = []
    for i, name in enumerate((RHO, M0, M1, M2, ENE)):
        if name == RHO:
            both = low[M0 + along] + high[M0 + along]
        elif name == ENE:
            both = vl * (low[ENE] + low[PRS]) + vh * (high[ENE] + high[PRS])
        else:
            both = vl * low[name] + vh * high[name]
            if i == 1 + along:
                both = both + (low[PRS] + high[PRS])
        out.append(half * (both - speed * (high[name] - low[name])))
    return out


def plane_kernel(density, velocity, pressure, code, far_ref, near_ref):
    odd = lax.rem(lax.axis_index("slab"), 2)
    for target, at in ((far_ref, odd), (near_ref, 1 - odd)):
        target[0] = density[at]
        for k in range(3):
            target[1 + k] = velocity[k, at]
        target[4] = pressure[at]
        target[5] = code[at].astype(F32) * (1.0 / 16.0)


def scatter(hot, third_hot, row):
    left = jnp.concatenate([hot * part.astype(BF16) for part in split3(row)], axis=0)
    found = lax.dot_general(
        left, third_hot[...], (((1,), (1,)), ((), ())), preferred_element_type=F32
    )
    n = hot.shape[0]
    return found[:n] + found[n : 2 * n] + found[2 * n :]


def inner_kernel(
    density, velocity, pressure, code, normal, weight, third_hot, plane_hot, source, total, terms
):
    hot = plane_hot[...]
    for k in range(3):
        source[k] = scatter(hot, third_hot, weight[...] * normal[k, 0]).reshape(density.shape)
    block_x, block_y, block_z = density.shape
    lane = lax.broadcasted_iota(I32, (TILE, block_z), 1)
    row = lax.broadcasted_iota(I32, (TILE, block_z), 0)
    tiles = block_y // TILE

    def prims(x, t):
        at = slice(t * TILE, (t + 1) * TILE)
        out = [density[x, at]] + [velocity[k, x, at] for k in range(3)]
        return out + [pressure[x, at], code[x, at].astype(F32) * (1.0 / 16.0)]

    def shifted(value, after):
        return jnp.where(row == TILE - 1, pltpu.roll(after, TILE - 1, 0), pltpu.roll(value, TILE - 1, 0))

    def full(x, t):
        own = prims(x, t)
        return dict(enumerate(own + list(derive(*own[:5]))))

    def keep(x, t, own):
        at = slice(t * TILE, (t + 1) * TILE)
        for i, name in enumerate((M0, M1, M2, ENE, SND)):
            terms[i, x, at] = own[name]

    for t in range(tiles):
        low, high = full(0, t), full(1, t)
        keep(0, t, low)
        keep(1, t, high)
        across = face(0, low, high)
        at = slice(t * TILE, (t + 1) * TILE)
        for x, own in ((0, low), (1, high)):
            right = {name: pltpu.roll(value, block_z - 1, 1) for name, value in own.items()}
            right[FRAC] = jnp.where(lane == block_z - 1, 0.0, right[FRAC])
            upper = face(2, own, right)
            for i in range(5):
                value = upper[i] - pltpu.roll(upper[i], 1, 1)
                total[i, x, at] = value + across[i] if x == 0 else value - across[i]
    for x in range(block_x):
        before = None
        for t in range(tiles):
            at = slice(t * TILE, (t + 1) * TILE)

            def load(u):
                at = slice(u * TILE, (u + 1) * TILE)
                out = {RHO: density[x, at], V1: velocity[1, x, at], PRS: pressure[x, at]}
                out[FRAC] = code[x, at].astype(F32) * (1.0 / 16.0)
                for i, name in enumerate((M0, M1, M2, ENE, SND)):
                    out[name] = terms[i, x, at]
                return out

            own = load(t)
            after = load(min(t + 1, tiles - 1))
            above = {name: shifted(own[name], after[name]) for name in own}
            if t == tiles - 1:
                above[FRAC] = jnp.where(row == TILE - 1, 0.0, above[FRAC])
            upper = face(1, own, above)
            turned = [pltpu.roll(value, 1, 0) for value in upper]
            for i in range(5):
                first = jnp.zeros_like(turned[i]) if before is None else before[i]
                total[i, x, at] += upper[i] - jnp.where(row == 0, first, turned[i])
            before = turned


def other(prims, fraction):
    live = fraction > 0.0
    prims = [jnp.where(live, prims[0], 1.0)] + prims[1:4] + [jnp.where(live, prims[4], 1.0)]
    return dict(enumerate(prims + [fraction] + list(derive(*prims))))


def outer_kernel(
    density, velocity, pressure, code, pushed, total, terms, far_ref, near_ref, most, scale_ref
):
    block_x, block_y, block_z = density.shape
    odd = lax.rem(lax.axis_index("slab"), 2)
    for x in range(block_x):
        use_near = odd == (1 - x)
        for t in range(block_y // TILE):
            at = slice(t * TILE, (t + 1) * TILE)
            got = [jnp.where(use_near, near_ref[f, at], far_ref[f, at]) for f in range(6)]
            beyond = other(got[:5], got[5])
            own = {RHO: density[x, at], PRS: pressure[x, at], V0: velocity[0, x, at]}
            for k in range(3):
                own[M0 + k] = terms[k, x, at]
            own[FRAC] = code[x, at].astype(F32) * (1.0 / 16.0)
            own[ENE], own[SND] = terms[3, x, at], terms[4, x, at]
            flux = face(0, beyond, own) if x == 0 else face(0, own, beyond)
            scale = step_ratio / own[FRAC]
            scale_ref[x, at] = scale
            for i, name in enumerate((RHO, M0, M1, M2, ENE)):
                change = total[i, x, at] - flux[i] if x == 0 else total[i, x, at] + flux[i]
                if 0 < i < 4:
                    change = change - pushed[i - 1, x, at]
                most[i, x, at] = own[name] - scale * change


def step_kernel(
    density,
    velocity,
    pressure,
    code,
    normal,
    mass,
    removed,
    motion,
    terms,
    most,
    scale_ref,
    message,
    weight_ref,
    third_hot,
    plane_hot,
    element_hot,
    state_out,
    motion_out,
    state,
    own_motion,
    sems,
):
    block_x, block_y, block_z = density.shape
    group = mass.shape[1]
    share = motion_out.shape[2]
    cols = message.shape[0]
    col = lax.axis_index("col")
    tiles = block_y // TILE
    copies = []

    def send(source, target):
        copies.append(pltpu.make_async_copy(source, target, sems.at[len(copies)]))
        copies[-1].start()

    for x in range(block_x):
        at = slice(TILE, block_y - TILE)
        send(most.at[0:4, x, at], state_out.at[0:4, x, at])

    keep = 1.0 - removed[...].astype(F32)
    quarters = group // LANES
    rows = slice(LOADS_AT, MESSAGE_ROWS)
    loads = message[0, rows]
    for j in range(1, cols):
        loads = loads + message[j, rows]
    new = []
    for k in range(3):
        at = quarters * k
        load = jnp.concatenate([loads[at + q : at + q + 1] for q in range(quarters)], axis=1)
        new.append((motion[k] + struct_step * load / mass[...]) * keep)
    split = [split3(value) for value in new]
    stacked = stack_rows([split[k][i] for i in range(3) for k in range(3)], 16).astype(BF16)
    moved = jnp.dot(stacked, element_hot[...], preferred_element_type=F32)
    work = jnp.zeros_like(weight_ref[...])
    for k in range(3):
        row = moved[k : k + 1] + moved[3 + k : 4 + k] + moved[6 + k : 7 + k]
        work = work + normal[k, 0] * row
    found = scatter(plane_hot[...], third_hot, weight_ref[...] * work)

    def edge(along_y):
        out = {RHO: density[:, along_y], PRS: pressure[:, along_y]}
        for k in range(3):
            out[V0 + k] = velocity[k, :, along_y]
            out[M0 + k] = terms[k, :, along_y]
        out[FRAC] = code[:, along_y].astype(F32) * (1.0 / 16.0)
        out[ENE], out[SND] = terms[3, :, along_y], terms[4, :, along_y]
        return out

    def arrived(j, inside):
        got = []
        for f in range(6):
            at = 2 * f * block_x
            low, high = message[j, at : at + block_x], message[j, at + block_x : at + 2 * block_x]
            got.append(jnp.concatenate([low, high], axis=1))
        return other(got[:5], jnp.where(inside, got[5], 0.0))

    bottom = face(1, arrived(jnp.maximum(col - 1, 0), col > 0), edge(0))
    top = face(1, edge(block_y - 1), arrived(jnp.minimum(col + 1, cols - 1), col < cols - 1))
    row = lax.broadcasted_iota(I32, (TILE, block_z), 0)

    def corrected(i, x, t):
        at = slice(t * TILE, (t + 1) * TILE)
        value = most[i, x, at]
        if t == 0:
            value = value + jnp.where(row == 0, scale_ref[x, at] * bottom[i][x : x + 1], 0.0)
        if t == tiles - 1:
            value = value - jnp.where(row == TILE - 1, scale_ref[x, at] * top[i][x : x + 1], 0.0)
        return value

    for x in range(block_x):
        for t in (0, tiles - 1):
            at = slice(t * TILE, (t + 1) * TILE)
            for i in range(4):
                state[i, x, at] = corrected(i, x, t)
            send(state.at[0:4, x, at], state_out.at[0:4, x, at])
    for k in range(3):
        own = new[k][:, 0:share]
        for j in range(1, cols):
            own = jnp.where(col == j, new[k][:, j * share : (j + 1) * share], own)
        own_motion[k] = own
    send(own_motion, motion_out)
    for x in range(block_x):
        for t in range(tiles):
            at = slice(t * TILE, (t + 1) * TILE)
            first = x * block_y + t * TILE
            state[4, x, at] = corrected(4, x, t) + scale_ref[x, at] * found[first : first + TILE]
    send(state.at[4], state_out.at[4])
    for copy in copies:
        copy.wait()


def in_vmem(*arrays):
    return [pltpu.with_memory_space_constraint(array, pltpu.VMEM) for array in arrays]


def in_hbm(*arrays):
    return [pltpu.with_memory_space_constraint(array, pltpu.HBM) for array in arrays]


def local(
    density,
    velocity,
    pressure,
    fraction_code,
    interface_cell,
    interface_element,
    interface_count,
    wall_normal,
    element_mass,
    element_removed,
    element_velocity,
):
    block_x, block_y, block_z = density.shape
    rows = interface_cell.shape[2]
    group = element_mass.shape[1]
    slabs, cols = lax.axis_size("slab"), lax.axis_size("col")
    share = group // cols
    vmem = pl.BlockSpec(memory_space=pltpu.VMEM)
    hbm = pl.BlockSpec(memory_space=pltpu.HBM)
    given = (
        density,
        velocity,
        pressure,
        fraction_code,
        wall_normal,
        element_mass,
        element_removed,
        element_velocity,
    )
    results = pl.pallas_call(
        gather_kernel,
        out_shape=tuple(pltpu.VMEM(array.shape, array.dtype) for array in given)
        + (
            jax.ShapeDtypeStruct((cols, MESSAGE_ROWS, LANES), F32),
            pltpu.VMEM((1, rows), F32),
            pltpu.VMEM((block_z, rows), BF16),
            pltpu.VMEM((block_x * block_y, rows), BF16),
            pltpu.VMEM((group, rows), BF16),
        ),
        in_specs=[pl.BlockSpec(memory_space=pl.ANY)] + [hbm] * 10,
        out_specs=[vmem] * 8 + [hbm] + [vmem] * 4,
        scratch_shapes=[
            pltpu.VMEM(interface_count.shape, I32),
            pltpu.VMEM(interface_cell.shape, I32),
            pltpu.VMEM(interface_element.shape, I32),
            pltpu.VMEM((cols, MESSAGE_ROWS, LANES), F32),
            pltpu.SemaphoreType.DMA((11,)),
            pltpu.SemaphoreType.DMA((2,)),
        ],
        compiler_params=pltpu.CompilerParams(vmem_limit_bytes=VMEM_BYTES),
        name="gather_rows",
    )(
        interface_count,
        *in_hbm(interface_cell, interface_element, *given),
    )
    kept, message, hots = results[:8], results[8], results[9:]

    message_in = lax.all_to_all(message, "col", 0, 0)
    planes = pltpu.VMEM((6, block_y, block_z), F32)
    far, near = pl.pallas_call(
        plane_kernel,
        out_shape=(planes, planes),
        in_specs=[vmem] * 4,
        out_specs=[vmem] * 2,
        cost_estimate=pl.CostEstimate(flops=100000, bytes_accessed=100000, transcendentals=0),
        compiler_params=pltpu.CompilerParams(vmem_limit_bytes=VMEM_BYTES),
        name="pack_planes",
    )(*in_vmem(*kept[:4]))
    pushed, total, terms = pl.pallas_call(
        inner_kernel,
        out_shape=(
            pltpu.VMEM((3, block_x, block_y, block_z), F32),
            pltpu.VMEM((5, block_x, block_y, block_z), F32),
            pltpu.VMEM((5, block_x, block_y, block_z), F32),
        ),
        in_specs=[vmem] * 8,
        out_specs=[vmem] * 3,
        cost_estimate=pl.CostEstimate(flops=10000000000, bytes_accessed=100000000, transcendentals=0),
        compiler_params=pltpu.CompilerParams(vmem_limit_bytes=VMEM_BYTES),
        name="inner_faces",
    )(*in_vmem(*kept[:5], *hots[:3]))
    inner = [(i, i ^ 1) for i in range(slabs)]
    outer = [(i, i + 1 if i % 2 else i - 1) for i in range(1, slabs - 1)]
    far_in = lax.ppermute(far, "slab", outer)
    near_in = lax.ppermute(near, "slab", inner)

    cells = in_vmem(*kept[:4])
    most, scale = pl.pallas_call(
        outer_kernel,
        out_shape=(
            pltpu.VMEM((5, block_x, block_y, block_z), F32),
            pltpu.VMEM((block_x, block_y, block_z), F32),
        ),
        in_specs=[vmem] * 9,
        out_specs=[vmem] * 2,
        cost_estimate=pl.CostEstimate(
            flops=100 * density.size, bytes_accessed=64 * density.size, transcendentals=0
        ),
        compiler_params=pltpu.CompilerParams(vmem_limit_bytes=VMEM_BYTES),
        name="outer_faces",
    )(*cells, *in_vmem(pushed, total, terms, far_in, near_in))
    state, new_motion = pl.pallas_call(
        step_kernel,
        out_shape=(
            jax.ShapeDtypeStruct((5, block_x, block_y, block_z), F32),
            jax.ShapeDtypeStruct((3, 1, share), F32),
        ),
        in_specs=[vmem] * 16,
        out_specs=[hbm, hbm],
        scratch_shapes=[
            pltpu.VMEM((5, block_x, block_y, block_z), F32),
            pltpu.VMEM((3, 1, share), F32),
            pltpu.SemaphoreType.DMA((3 * block_x + 2,)),
        ],
        compiler_params=pltpu.CompilerParams(vmem_limit_bytes=VMEM_BYTES),
        name="step_cells",
    )(*in_vmem(*kept, terms, most, scale, message_in, *hots))
    return (state, new_motion)


def solution(mesh):
    placed = (
        P("slab", "col", None),
        P(None, "slab", "col", None),
        P("slab", "col", None),
        P("slab", "col", None),
        P("slab", "col", None),
        P("slab", "col", None),
        P("slab", "col"),
        P(None, "slab", "col", None),
        P("slab", None),
        P("slab", None),
        P(None, "slab", None),
    )
    return jax.shard_map(
        local,
        mesh=mesh,
        in_specs=placed,
        out_specs=(P(None, "slab", "col", None), P(None, "slab", "col")),
        check_vma=False,
    )
```

```python
import jax
import jax.numpy as jnp
from jax import lax
from jax.experimental import pallas as pl
from jax.experimental.pallas import tpu as pltpu
from jax.sharding import PartitionSpec as P

ratio_heat = 1.4
step_ratio = 0.1
struct_step = 1.0

F32, BF16, I32 = jnp.float32, jnp.bfloat16, jnp.int32
ORDER = (0, 2, 3, 1)
VMEM_BYTES = 8 * 2**20
TILE = 8
LANES = 128
LOADS_AT = 24
MESSAGE_ROWS = 40
QUARTERS = 4


def split3(value):
    high = value.astype(BF16).astype(F32)
    rest = value - high
    middle = rest.astype(BF16).astype(F32)
    return high, middle, rest - middle


def gather_kernel(count_in, cell_in, element_in, *refs):
    given, kept = refs[:8], refs[8:16]
    message_out, weight_ref, third_hot, plane_hot, low_hot, pull_ref = refs[16:22]
    count, cell, element, message, sems, sent = refs[22:]
    density, velocity, pressure, code, normal = kept[:5]
    pairs = [(cell_in, cell), (element_in, element), (count_in, count)]
    pairs += [(given[i], kept[i]) for i in (2, 3, 4, 0, 1, 5, 6, 7)]
    copies = [pltpu.make_async_copy(a, b, sems.at[i]) for i, (a, b) in enumerate(pairs)]
    for copy in copies:
        copy.start()
    block_x, block_y, block_z = density.shape
    rows = cell.shape[2]
    col = lax.axis_index("col")

    copies[0].wait()
    copies[1].wait()
    place = cell[0]
    third = jnp.bitwise_and(place, block_z - 1)
    plane = lax.shift_right_logical(place, block_z.bit_length() - 1)
    third_mask = lax.broadcasted_iota(I32, (block_z, rows), 0) == third
    third_hot[...] = jnp.where(third_mask, 1.0, 0.0).astype(BF16)
    plane_mask = lax.broadcasted_iota(I32, (block_x * block_y, rows), 0) == plane
    plane_hot[...] = jnp.where(plane_mask, 1.0, 0.0).astype(BF16)
    low_mask = lax.broadcasted_iota(I32, (LANES, rows), 0) == jnp.bitwise_and(element[0], LANES - 1)
    low_hot[...] = jnp.where(low_mask, 1.0, 0.0).astype(BF16)
    for copy in copies[2:6]:
        copy.wait()
    line = lax.broadcasted_iota(I32, (16, rows), 0)
    high = lax.shift_right_logical(element[0], LANES.bit_length() - 1)
    pull = jnp.zeros((16, rows), F32)
    for k in range(3):
        pull = jnp.where(line == high + QUARTERS * k, normal[k, 0], pull)
    pull_ref[...] = pull
    fraction = code[...].astype(F32) * (1.0 / 16.0)
    table = (pressure[...] * (1.0 - fraction)).reshape(block_x * block_y, block_z)
    parts = jnp.concatenate(split3(table), axis=0).astype(BF16)
    found = jnp.dot(parts, third_hot[...], preferred_element_type=F32)
    n = block_x * block_y
    found = found[:n] + found[n : 2 * n] + found[2 * n :]
    found = jnp.sum(jnp.where(plane_mask, found, 0.0), axis=0, keepdims=True)
    live = lax.broadcasted_iota(I32, (1, rows), 1) < count[...]
    weight = jnp.where(live, found, 0.0)
    weight_ref[...] = weight

    for copy in copies[6:]:
        copy.wait()
    def edge(x, y):
        out = [density[x, y : y + 1]]
        out += [velocity[k, x, y : y + 1] for k in range(3)]
        out += [pressure[x, y : y + 1], code[x, y : y + 1].astype(F32) * (1.0 / 16.0)]
        return out

    for x in range(block_x):
        first, last = edge(x, 0), edge(x, block_y - 1)
        for j in range(message.shape[0]):
            for f in range(6):
                row = jnp.where(col < ORDER[j], last[f], first[f])
                for h in range(2):
                    at = (2 * f + h) * block_x + x
                    message[j, at : at + 1] = row[:, h * LANES : (h + 1) * LANES]
    edges = slice(0, LOADS_AT)
    edge_copy = pltpu.make_async_copy(message.at[:, edges], message_out.at[:, edges], sent.at[0])
    edge_copy.start()

    force = jnp.concatenate(split3(-weight * pull), axis=0).astype(BF16)
    partial = lax.dot_general(
        force, low_hot[...], (((1,), (1,)), ((), ())), preferred_element_type=F32
    )
    partial = partial[:16] + partial[16:32] + partial[32:]
    for j in range(message.shape[0]):
        message[j, LOADS_AT:] = partial
    loads = slice(LOADS_AT, MESSAGE_ROWS)
    load_copy = pltpu.make_async_copy(message.at[:, loads], message_out.at[:, loads], sent.at[1])
    load_copy.start()
    edge_copy.wait()
    load_copy.wait()


def derive(density, v0, v1, v2, pressure):
    m0, m1, m2 = density * v0, density * v1, density * v2
    energy = pressure * (1.0 / 0.4) + 0.5 * density * (v0 * v0 + v1 * v1 + v2 * v2)
    sound = jnp.sqrt(ratio_heat * pressure / density)
    return m0, m1, m2, energy, sound


RHO, V0, V1, V2, PRS, FRAC, M0, M1, M2, ENE, SND = range(11)


def face(along, low, high):
    vl, vh = low[V0 + along], high[V0 + along]
    speed = jnp.maximum(jnp.abs(vl) + low[SND], jnp.abs(vh) + high[SND])
    half = 0.5 * jnp.minimum(low[FRAC], high[FRAC])
    out = []
    for i, name in enumerate((RHO, M0, M1, M2, ENE)):
        if name == RHO:
            both = low[M0 + along] + high[M0 + along]
        elif name == ENE:
            both = vl * (low[ENE] + low[PRS]) + vh * (high[ENE] + high[PRS])
        else:
            both = vl * low[name] + vh * high[name]
            if i == 1 + along:
                both = both + (low[PRS] + high[PRS])
        out.append(half * (both - speed * (high[name] - low[name])))
    return out


def plane_kernel(density, velocity, pressure, code, far_ref, near_ref):
    odd = lax.rem(lax.axis_index("slab"), 2)
    for target, at in ((far_ref, odd), (near_ref, 1 - odd)):
        target[0] = density[at]
        for k in range(3):
            target[1 + k] = velocity[k, at]
        target[4] = pressure[at]
        target[5] = code[at].astype(F32) * (1.0 / 16.0)


def scatter(hot, third_hot, row):
    left = jnp.concatenate([hot * part.astype(BF16) for part in split3(row)], axis=0)
    found = lax.dot_general(
        left, third_hot[...], (((1,), (1,)), ((), ())), preferred_element_type=F32
    )
    n = hot.shape[0]
    return found[:n] + found[n : 2 * n] + found[2 * n :]


def inner_kernel(
    density,
    velocity,
    pressure,
    code,
    normal,
    mass,
    removed,
    motion,
    weight,
    third_hot,
    plane_hot,
    source,
    total,
    terms,
    element,
):
    element[...] = jnp.ones_like(element)
    for q in range(QUARTERS):
        at = slice(q * LANES, (q + 1) * LANES)
        kept = 1.0 - removed[:, at].astype(F32)
        for k in range(3):
            line = slice(QUARTERS * k + q, QUARTERS * k + q + 1)
            element[0, line] = mass[:, at]
            element[1, line] = kept
            element[2, line] = motion[k, :, at]
    hot = plane_hot[...]
    for k in range(3):
        source[k] = scatter(hot, third_hot, weight[...] * normal[k, 0]).reshape(density.shape)
    block_x, block_y, block_z = density.shape
    lane = lax.broadcasted_iota(I32, (TILE, block_z), 1)
    row = lax.broadcasted_iota(I32, (TILE, block_z), 0)
    tiles = block_y // TILE

    def prims(x, t):
        at = slice(t * TILE, (t + 1) * TILE)
        out = [density[x, at]] + [velocity[k, x, at] for k in range(3)]
        return out + [pressure[x, at], code[x, at].astype(F32) * (1.0 / 16.0)]

    def shifted(value, after):
        return jnp.where(row == TILE - 1, pltpu.roll(after, TILE - 1, 0), pltpu.roll(value, TILE - 1, 0))

    def full(x, t):
        own = prims(x, t)
        return dict(enumerate(own + list(derive(*own[:5]))))

    def keep(x, t, own):
        at = slice(t * TILE, (t + 1) * TILE)
        for i, name in enumerate((M0, M1, M2, ENE, SND)):
            terms[i, x, at] = own[name]

    for t in range(tiles):
        low, high = full(0, t), full(1, t)
        keep(0, t, low)
        keep(1, t, high)
        across = face(0, low, high)
        at = slice(t * TILE, (t + 1) * TILE)
        for x, own in ((0, low), (1, high)):
            right = {name: pltpu.roll(value, block_z - 1, 1) for name, value in own.items()}
            right[FRAC] = jnp.where(lane == block_z - 1, 0.0, right[FRAC])
            upper = face(2, own, right)
            for i in range(5):
                value = upper[i] - pltpu.roll(upper[i], 1, 1)
                total[i, x, at] = value + across[i] if x == 0 else value - across[i]
    for x in range(block_x):
        before = None
        for t in range(tiles):
            at = slice(t * TILE, (t + 1) * TILE)

            def load(u):
                at = slice(u * TILE, (u + 1) * TILE)
                out = {RHO: density[x, at], V1: velocity[1, x, at], PRS: pressure[x, at]}
                out[FRAC] = code[x, at].astype(F32) * (1.0 / 16.0)
                for i, name in enumerate((M0, M1, M2, ENE, SND)):
                    out[name] = terms[i, x, at]
                return out

            own = load(t)
            after = load(min(t + 1, tiles - 1))
            above = {name: shifted(own[name], after[name]) for name in own}
            if t == tiles - 1:
                above[FRAC] = jnp.where(row == TILE - 1, 0.0, above[FRAC])
            upper = face(1, own, above)
            turned = [pltpu.roll(value, 1, 0) for value in upper]
            for i in range(5):
                first = jnp.zeros_like(turned[i]) if before is None else before[i]
                total[i, x, at] += upper[i] - jnp.where(row == 0, first, turned[i])
            before = turned


def other(prims, fraction):
    live = fraction > 0.0
    prims = [jnp.where(live, prims[0], 1.0)] + prims[1:4] + [jnp.where(live, prims[4], 1.0)]
    return dict(enumerate(prims + [fraction] + list(derive(*prims))))


def outer_kernel(
    density, velocity, pressure, code, pushed, total, terms, far_ref, near_ref, most, scale_ref
):
    block_x, block_y, block_z = density.shape
    odd = lax.rem(lax.axis_index("slab"), 2)
    for x in range(block_x):
        use_near = odd == (1 - x)
        for t in range(block_y // TILE):
            at = slice(t * TILE, (t + 1) * TILE)
            got = [jnp.where(use_near, near_ref[f, at], far_ref[f, at]) for f in range(6)]
            beyond = other(got[:5], got[5])
            own = {RHO: density[x, at], PRS: pressure[x, at], V0: velocity[0, x, at]}
            for k in range(3):
                own[M0 + k] = terms[k, x, at]
            own[FRAC] = code[x, at].astype(F32) * (1.0 / 16.0)
            own[ENE], own[SND] = terms[3, x, at], terms[4, x, at]
            flux = face(0, beyond, own) if x == 0 else face(0, own, beyond)
            scale = step_ratio / own[FRAC]
            scale_ref[x, at] = scale
            for i, name in enumerate((RHO, M0, M1, M2, ENE)):
                change = total[i, x, at] - flux[i] if x == 0 else total[i, x, at] + flux[i]
                if 0 < i < 4:
                    change = change - pushed[i - 1, x, at]
                most[i, x, at] = own[name] - scale * change


def step_kernel(
    density,
    velocity,
    pressure,
    code,
    terms,
    element,
    most,
    scale_ref,
    message,
    weight_ref,
    third_hot,
    plane_hot,
    low_hot,
    pull_ref,
    state_out,
    motion_out,
    state,
    own_motion,
    sems,
):
    block_x, block_y, block_z = density.shape
    cols = message.shape[0]
    col = lax.axis_index("col")
    tiles = block_y // TILE
    copies = []

    def send(source, target):
        copies.append(pltpu.make_async_copy(source, target, sems.at[len(copies)]))
        copies[-1].start()

    for x in range(block_x):
        at = slice(TILE, block_y - TILE)
        send(most.at[0:4, x, at], state_out.at[0:4, x, at])

    rows = slice(LOADS_AT, MESSAGE_ROWS)
    loads = message[0, rows]
    for j in range(1, cols):
        loads = loads + message[j, rows]
    new = (element[2] + struct_step * loads / element[0]) * element[1]
    parts = jnp.concatenate(split3(new), axis=0).astype(BF16)
    moved = jnp.dot(parts, low_hot[...], preferred_element_type=F32)
    moved = moved[:16] + moved[16:32] + moved[32:]
    work = jnp.sum(pull_ref[...] * moved, axis=0, keepdims=True)
    found = scatter(plane_hot[...], third_hot, weight_ref[...] * work)

    def edge(along_y):
        out = {RHO: density[:, along_y], PRS: pressure[:, along_y]}
        for k in range(3):
            out[V0 + k] = velocity[k, :, along_y]
            out[M0 + k] = terms[k, :, along_y]
        out[FRAC] = code[:, along_y].astype(F32) * (1.0 / 16.0)
        out[ENE], out[SND] = terms[3, :, along_y], terms[4, :, along_y]
        return out

    def arrived(beside, inside):
        j = sum(jnp.where(beside == c, place, 0) for place, c in enumerate(ORDER))
        got = []
        for f in range(6):
            at = 2 * f * block_x
            low, high = message[j, at : at + block_x], message[j, at + block_x : at + 2 * block_x]
            got.append(jnp.concatenate([low, high], axis=1))
        return other(got[:5], jnp.where(inside, got[5], 0.0))

    bottom = face(1, arrived(jnp.maximum(col - 1, 0), col > 0), edge(0))
    top = face(1, edge(block_y - 1), arrived(jnp.minimum(col + 1, cols - 1), col < cols - 1))
    row = lax.broadcasted_iota(I32, (TILE, block_z), 0)

    def corrected(i, x, t):
        at = slice(t * TILE, (t + 1) * TILE)
        value = most[i, x, at]
        if t == 0:
            value = value + jnp.where(row == 0, scale_ref[x, at] * bottom[i][x : x + 1], 0.0)
        if t == tiles - 1:
            value = value - jnp.where(row == TILE - 1, scale_ref[x, at] * top[i][x : x + 1], 0.0)
        return value

    for x in range(block_x):
        for t in (0, tiles - 1):
            at = slice(t * TILE, (t + 1) * TILE)
            for i in range(4):
                state[i, x, at] = corrected(i, x, t)
            send(state.at[0:4, x, at], state_out.at[0:4, x, at])
    for k in range(3):
        own = new[QUARTERS * k : QUARTERS * k + 1]
        for j in range(1, cols):
            at = QUARTERS * k + j
            own = jnp.where(col == j, new[at : at + 1], own)
        own_motion[k] = own
    send(own_motion, motion_out)
    for x in range(block_x):
        for t in range(tiles):
            at = slice(t * TILE, (t + 1) * TILE)
            first = x * block_y + t * TILE
            state[4, x, at] = corrected(4, x, t) + scale_ref[x, at] * found[first : first + TILE]
    send(state.at[4], state_out.at[4])
    for copy in copies:
        copy.wait()


def in_vmem(*arrays):
    return [pltpu.with_memory_space_constraint(array, pltpu.VMEM) for array in arrays]


def in_hbm(*arrays):
    return [pltpu.with_memory_space_constraint(array, pltpu.HBM) for array in arrays]


def local(
    density,
    velocity,
    pressure,
    fraction_code,
    interface_cell,
    interface_element,
    interface_count,
    wall_normal,
    element_mass,
    element_removed,
    element_velocity,
):
    block_x, block_y, block_z = density.shape
    rows = interface_cell.shape[2]
    group = element_mass.shape[1]
    slabs, cols = lax.axis_size("slab"), lax.axis_size("col")
    share = group // cols
    vmem = pl.BlockSpec(memory_space=pltpu.VMEM)
    hbm = pl.BlockSpec(memory_space=pltpu.HBM)
    given = (
        density,
        velocity,
        pressure,
        fraction_code,
        wall_normal,
        element_mass,
        element_removed,
        element_velocity,
    )
    results = pl.pallas_call(
        gather_kernel,
        out_shape=tuple(pltpu.VMEM(array.shape, array.dtype) for array in given)
        + (
            jax.ShapeDtypeStruct((cols, MESSAGE_ROWS, LANES), F32),
            pltpu.VMEM((1, rows), F32),
            pltpu.VMEM((block_z, rows), BF16),
            pltpu.VMEM((block_x * block_y, rows), BF16),
            pltpu.VMEM((LANES, rows), BF16),
            pltpu.VMEM((16, rows), F32),
        ),
        in_specs=[pl.BlockSpec(memory_space=pl.ANY)] + [hbm] * 10,
        out_specs=[vmem] * 8 + [hbm] + [vmem] * 5,
        scratch_shapes=[
            pltpu.VMEM(interface_count.shape, I32),
            pltpu.VMEM(interface_cell.shape, I32),
            pltpu.VMEM(interface_element.shape, I32),
            pltpu.VMEM((cols, MESSAGE_ROWS, LANES), F32),
            pltpu.SemaphoreType.DMA((11,)),
            pltpu.SemaphoreType.DMA((2,)),
        ],
        compiler_params=pltpu.CompilerParams(vmem_limit_bytes=VMEM_BYTES),
        name="gather_rows",
    )(
        interface_count,
        *in_hbm(interface_cell, interface_element, *given),
    )
    kept, message, hots = results[:8], results[8], results[9:]

    message_in = lax.all_to_all(
        message, "col", 0, 0, axis_index_groups=[list(ORDER)]
    )
    planes = pltpu.VMEM((6, block_y, block_z), F32)
    far, near = pl.pallas_call(
        plane_kernel,
        out_shape=(planes, planes),
        in_specs=[vmem] * 4,
        out_specs=[vmem] * 2,
        cost_estimate=pl.CostEstimate(flops=100000, bytes_accessed=100000, transcendentals=0),
        compiler_params=pltpu.CompilerParams(vmem_limit_bytes=VMEM_BYTES),
        name="pack_planes",
    )(*in_vmem(*kept[:4]))
    pushed, total, terms, elements = pl.pallas_call(
        inner_kernel,
        out_shape=(
            pltpu.VMEM((3, block_x, block_y, block_z), F32),
            pltpu.VMEM((5, block_x, block_y, block_z), F32),
            pltpu.VMEM((5, block_x, block_y, block_z), F32),
            pltpu.VMEM((3, 16, LANES), F32),
        ),
        in_specs=[vmem] * 11,
        out_specs=[vmem] * 4,
        cost_estimate=pl.CostEstimate(flops=10000000000, bytes_accessed=100000000, transcendentals=0),
        compiler_params=pltpu.CompilerParams(vmem_limit_bytes=VMEM_BYTES),
        name="inner_faces",
    )(*in_vmem(*kept, *hots[:3]))
    inner = [(i, i ^ 1) for i in range(slabs)]
    outer = [(i, i + 1 if i % 2 else i - 1) for i in range(1, slabs - 1)]
    far_in = lax.ppermute(far, "slab", outer)
    near_in = lax.ppermute(near, "slab", inner)

    cells = in_vmem(*kept[:4])
    most, scale = pl.pallas_call(
        outer_kernel,
        out_shape=(
            pltpu.VMEM((5, block_x, block_y, block_z), F32),
            pltpu.VMEM((block_x, block_y, block_z), F32),
        ),
        in_specs=[vmem] * 9,
        out_specs=[vmem] * 2,
        cost_estimate=pl.CostEstimate(
            flops=100 * density.size, bytes_accessed=64 * density.size, transcendentals=0
        ),
        compiler_params=pltpu.CompilerParams(vmem_limit_bytes=VMEM_BYTES),
        name="outer_faces",
    )(*cells, *in_vmem(pushed, total, terms, far_in, near_in))
    state, new_motion = pl.pallas_call(
        step_kernel,
        out_shape=(
            jax.ShapeDtypeStruct((5, block_x, block_y, block_z), F32),
            jax.ShapeDtypeStruct((3, 1, share), F32),
        ),
        in_specs=[vmem] * 14,
        out_specs=[hbm, hbm],
        scratch_shapes=[
            pltpu.VMEM((5, block_x, block_y, block_z), F32),
            pltpu.VMEM((3, 1, share), F32),
            pltpu.SemaphoreType.DMA((3 * block_x + 2,)),
        ],
        compiler_params=pltpu.CompilerParams(vmem_limit_bytes=VMEM_BYTES),
        name="step_cells",
    )(*in_vmem(*kept[:4], terms, elements, most, scale, message_in, *hots))
    return (state, new_motion)


def solution(mesh):
    placed = (
        P("slab", "col", None),
        P(None, "slab", "col", None),
        P("slab", "col", None),
        P("slab", "col", None),
        P("slab", "col", None),
        P("slab", "col", None),
        P("slab", "col"),
        P(None, "slab", "col", None),
        P("slab", None),
        P("slab", None),
        P(None, "slab", None),
    )
    return jax.shard_map(
        local,
        mesh=mesh,
        in_specs=placed,
        out_specs=(P(None, "slab", "col", None), P(None, "slab", "col")),
        check_vma=False,
    )
```

```python
import jax
import jax.numpy as jnp
from jax import lax
from jax.experimental import pallas as pl
from jax.experimental.pallas import tpu as pltpu
from jax.sharding import PartitionSpec as P

ratio_heat = 1.4
step_ratio = 0.1
struct_step = 1.0

F32, BF16, I32 = jnp.float32, jnp.bfloat16, jnp.int32
ORDER = (0, 2, 3, 1)
VMEM_BYTES = 8 * 2**20
TILE = 8
LANES = 128
LOADS_AT = 24
MESSAGE_ROWS = 40
QUARTERS = 4


def split3(value):
    high = value.astype(BF16).astype(F32)
    rest = value - high
    middle = rest.astype(BF16).astype(F32)
    return high, middle, rest - middle


def gather_kernel(count_in, cell_in, element_in, *refs):
    given, kept = refs[:8], refs[8:16]
    message_out, weight_ref, third_hot, plane_hot, low_hot, pull_ref = refs[16:22]
    count, cell, element, message, sems, sent = refs[22:]
    density, velocity, pressure, code, normal = kept[:5]
    pairs = [(cell_in, cell), (element_in, element), (count_in, count)]
    pairs += [(given[i], kept[i]) for i in (2, 3, 4, 0, 1, 5, 6, 7)]
    copies = [pltpu.make_async_copy(a, b, sems.at[i]) for i, (a, b) in enumerate(pairs)]
    for copy in copies:
        copy.start()
    block_x, block_y, block_z = density.shape
    rows = cell.shape[2]
    col = lax.axis_index("col")

    copies[0].wait()
    copies[1].wait()
    place = cell[0]
    third = jnp.bitwise_and(place, block_z - 1)
    plane = lax.shift_right_logical(place, block_z.bit_length() - 1)
    third_mask = lax.broadcasted_iota(I32, (block_z, rows), 0) == third
    third_hot[...] = jnp.where(third_mask, 1.0, 0.0).astype(BF16)
    plane_mask = lax.broadcasted_iota(I32, (block_x * block_y, rows), 0) == plane
    plane_hot[...] = jnp.where(plane_mask, 1.0, 0.0).astype(BF16)
    low_mask = lax.broadcasted_iota(I32, (LANES, rows), 0) == jnp.bitwise_and(element[0], LANES - 1)
    low_hot[...] = jnp.where(low_mask, 1.0, 0.0).astype(BF16)
    for copy in copies[2:6]:
        copy.wait()
    line = lax.broadcasted_iota(I32, (16, rows), 0)
    high = lax.shift_right_logical(element[0], LANES.bit_length() - 1)
    pull = jnp.zeros((16, rows), F32)
    for k in range(3):
        pull = jnp.where(line == high + QUARTERS * k, normal[k, 0], pull)
    pull_ref[...] = pull
    fraction = code[...].astype(F32) * (1.0 / 16.0)
    table = (pressure[...] * (1.0 - fraction)).reshape(block_x * block_y, block_z)
    parts = jnp.concatenate(split3(table), axis=0).astype(BF16)
    found = jnp.dot(parts, third_hot[...], preferred_element_type=F32)
    n = block_x * block_y
    found = found[:n] + found[n : 2 * n] + found[2 * n :]
    found = jnp.sum(jnp.where(plane_mask, found, 0.0), axis=0, keepdims=True)
    live = lax.broadcasted_iota(I32, (1, rows), 1) < count[...]
    weight = jnp.where(live, found, 0.0)
    weight_ref[...] = weight

    for copy in copies[6:]:
        copy.wait()
    def edge(x, y):
        out = [density[x, y : y + 1]]
        out += [velocity[k, x, y : y + 1] for k in range(3)]
        out += [pressure[x, y : y + 1], code[x, y : y + 1].astype(F32) * (1.0 / 16.0)]
        return out

    for x in range(block_x):
        first, last = edge(x, 0), edge(x, block_y - 1)
        for j in range(message.shape[0]):
            for f in range(6):
                row = jnp.where(col < ORDER[j], last[f], first[f])
                for h in range(2):
                    at = (2 * f + h) * block_x + x
                    message[j, at : at + 1] = row[:, h * LANES : (h + 1) * LANES]
    edges = slice(0, LOADS_AT)
    edge_copy = pltpu.make_async_copy(message.at[:, edges], message_out.at[:, edges], sent.at[0])
    edge_copy.start()

    force = jnp.concatenate(split3(-weight * pull), axis=0).astype(BF16)
    partial = lax.dot_general(
        force, low_hot[...], (((1,), (1,)), ((), ())), preferred_element_type=F32
    )
    partial = partial[:16] + partial[16:32] + partial[32:]
    for j in range(message.shape[0]):
        message[j, LOADS_AT:] = partial
    loads = slice(LOADS_AT, MESSAGE_ROWS)
    load_copy = pltpu.make_async_copy(message.at[:, loads], message_out.at[:, loads], sent.at[1])
    load_copy.start()
    edge_copy.wait()
    load_copy.wait()


def derive(density, v0, v1, v2, pressure):
    m0, m1, m2 = density * v0, density * v1, density * v2
    energy = pressure * (1.0 / 0.4) + 0.5 * density * (v0 * v0 + v1 * v1 + v2 * v2)
    sound = jnp.sqrt(ratio_heat * pressure / density)
    return m0, m1, m2, energy, sound


RHO, V0, V1, V2, PRS, FRAC, M0, M1, M2, ENE, SND = range(11)


def face(along, low, high):
    vl, vh = low[V0 + along], high[V0 + along]
    speed = jnp.maximum(jnp.abs(vl) + low[SND], jnp.abs(vh) + high[SND])
    half = 0.5 * jnp.minimum(low[FRAC], high[FRAC])
    out = []
    for i, name in enumerate((RHO, M0, M1, M2, ENE)):
        if name == RHO:
            both = low[M0 + along] + high[M0 + along]
        elif name == ENE:
            both = vl * (low[ENE] + low[PRS]) + vh * (high[ENE] + high[PRS])
        else:
            both = vl * low[name] + vh * high[name]
            if i == 1 + along:
                both = both + (low[PRS] + high[PRS])
        out.append(half * (both - speed * (high[name] - low[name])))
    return out


def plane_kernel(density, velocity, pressure, code, far_ref, near_ref):
    odd = lax.rem(lax.axis_index("slab"), 2)
    for target, at in ((far_ref, odd), (near_ref, 1 - odd)):
        target[0] = density[at]
        for k in range(3):
            target[1 + k] = velocity[k, at]
        target[4] = pressure[at]
        target[5] = code[at].astype(F32) * (1.0 / 16.0)


def scatter(hot, third_hot, row):
    left = jnp.concatenate([hot * part.astype(BF16) for part in split3(row)], axis=0)
    found = lax.dot_general(
        left, third_hot[...], (((1,), (1,)), ((), ())), preferred_element_type=F32
    )
    n = hot.shape[0]
    return found[:n] + found[n : 2 * n] + found[2 * n :]


def inner_kernel(
    density,
    velocity,
    pressure,
    code,
    normal,
    mass,
    removed,
    motion,
    weight,
    third_hot,
    plane_hot,
    source,
    total,
    terms,
    element,
):
    element[...] = jnp.ones_like(element)
    for q in range(QUARTERS):
        at = slice(q * LANES, (q + 1) * LANES)
        kept = 1.0 - removed[:, at].astype(F32)
        for k in range(3):
            line = slice(QUARTERS * k + q, QUARTERS * k + q + 1)
            element[0, line] = struct_step / mass[:, at]
            element[1, line] = kept
            element[2, line] = motion[k, :, at]
    hot = plane_hot[...]
    for k in range(3):
        source[k] = scatter(hot, third_hot, weight[...] * normal[k, 0]).reshape(density.shape)
    block_x, block_y, block_z = density.shape
    lane = lax.broadcasted_iota(I32, (TILE, block_z), 1)
    row = lax.broadcasted_iota(I32, (TILE, block_z), 0)
    tiles = block_y // TILE

    def prims(x, t):
        at = slice(t * TILE, (t + 1) * TILE)
        out = [density[x, at]] + [velocity[k, x, at] for k in range(3)]
        return out + [pressure[x, at], code[x, at].astype(F32) * (1.0 / 16.0)]

    def shifted(value, after):
        return jnp.where(row == TILE - 1, pltpu.roll(after, TILE - 1, 0), pltpu.roll(value, TILE - 1, 0))

    def full(x, t):
        own = prims(x, t)
        return dict(enumerate(own + list(derive(*own[:5]))))

    def keep(x, t, own):
        at = slice(t * TILE, (t + 1) * TILE)
        for i, name in enumerate((M0, M1, M2, ENE, SND)):
            terms[i, x, at] = own[name]

    for t in range(tiles):
        low, high = full(0, t), full(1, t)
        keep(0, t, low)
        keep(1, t, high)
        across = face(0, low, high)
        at = slice(t * TILE, (t + 1) * TILE)
        for x, own in ((0, low), (1, high)):
            right = {name: pltpu.roll(value, block_z - 1, 1) for name, value in own.items()}
            right[FRAC] = jnp.where(lane == block_z - 1, 0.0, right[FRAC])
            upper = face(2, own, right)
            for i in range(5):
                value = upper[i] - pltpu.roll(upper[i], 1, 1)
                total[i, x, at] = value + across[i] if x == 0 else value - across[i]
    for x in range(block_x):
        before = None
        for t in range(tiles):
            at = slice(t * TILE, (t + 1) * TILE)

            def load(u):
                at = slice(u * TILE, (u + 1) * TILE)
                out = {RHO: density[x, at], V1: velocity[1, x, at], PRS: pressure[x, at]}
                out[FRAC] = code[x, at].astype(F32) * (1.0 / 16.0)
                for i, name in enumerate((M0, M1, M2, ENE, SND)):
                    out[name] = terms[i, x, at]
                return out

            own = load(t)
            after = load(min(t + 1, tiles - 1))
            above = {name: shifted(own[name], after[name]) for name in own}
            if t == tiles - 1:
                above[FRAC] = jnp.where(row == TILE - 1, 0.0, above[FRAC])
            upper = face(1, own, above)
            turned = [pltpu.roll(value, 1, 0) for value in upper]
            for i in range(5):
                first = jnp.zeros_like(turned[i]) if before is None else before[i]
                total[i, x, at] += upper[i] - jnp.where(row == 0, first, turned[i])
            before = turned


def other(prims, fraction):
    live = fraction > 0.0
    prims = [jnp.where(live, prims[0], 1.0)] + prims[1:4] + [jnp.where(live, prims[4], 1.0)]
    return dict(enumerate(prims + [fraction] + list(derive(*prims))))


def outer_kernel(
    density, velocity, pressure, code, pushed, total, terms, far_ref, near_ref, most, scale_ref
):
    block_x, block_y, block_z = density.shape
    odd = lax.rem(lax.axis_index("slab"), 2)
    for x in range(block_x):
        use_near = odd == (1 - x)
        for t in range(block_y // TILE):
            at = slice(t * TILE, (t + 1) * TILE)
            got = [jnp.where(use_near, near_ref[f, at], far_ref[f, at]) for f in range(6)]
            beyond = other(got[:5], got[5])
            own = {RHO: density[x, at], PRS: pressure[x, at], V0: velocity[0, x, at]}
            for k in range(3):
                own[M0 + k] = terms[k, x, at]
            own[FRAC] = code[x, at].astype(F32) * (1.0 / 16.0)
            own[ENE], own[SND] = terms[3, x, at], terms[4, x, at]
            flux = face(0, beyond, own) if x == 0 else face(0, own, beyond)
            scale = step_ratio / own[FRAC]
            scale_ref[x, at] = scale
            for i, name in enumerate((RHO, M0, M1, M2, ENE)):
                change = total[i, x, at] - flux[i] if x == 0 else total[i, x, at] + flux[i]
                if 0 < i < 4:
                    change = change - pushed[i - 1, x, at]
                most[i, x, at] = own[name] - scale * change


def step_kernel(
    density,
    velocity,
    pressure,
    code,
    terms,
    element,
    most,
    scale_ref,
    message,
    weight_ref,
    third_hot,
    plane_hot,
    low_hot,
    pull_ref,
    state_out,
    motion_out,
    state,
    own_motion,
    sems,
):
    block_x, block_y, block_z = density.shape
    cols = message.shape[0]
    col = lax.axis_index("col")
    tiles = block_y // TILE
    copies = []

    def send(source, target):
        copies.append(pltpu.make_async_copy(source, target, sems.at[len(copies)]))
        copies[-1].start()

    at = slice(TILE, block_y - TILE)
    send(most.at[0:4, :, at], state_out.at[0:4, :, at])

    rows = slice(LOADS_AT, MESSAGE_ROWS)
    loads = message[0, rows]
    for j in range(1, cols):
        loads = loads + message[j, rows]
    new = (element[2] + loads * element[0]) * element[1]
    parts = jnp.concatenate(split3(new), axis=0).astype(BF16)
    moved = jnp.dot(parts, low_hot[...], preferred_element_type=F32)
    moved = moved[:16] + moved[16:32] + moved[32:]
    work = jnp.sum(pull_ref[...] * moved, axis=0, keepdims=True)
    found = scatter(plane_hot[...], third_hot, weight_ref[...] * work)

    def edge(along_y):
        out = {RHO: density[:, along_y], PRS: pressure[:, along_y]}
        for k in range(3):
            out[V0 + k] = velocity[k, :, along_y]
            out[M0 + k] = terms[k, :, along_y]
        out[FRAC] = code[:, along_y].astype(F32) * (1.0 / 16.0)
        out[ENE], out[SND] = terms[3, :, along_y], terms[4, :, along_y]
        return out

    def arrived(beside, inside):
        j = sum(jnp.where(beside == c, place, 0) for place, c in enumerate(ORDER))
        got = []
        for f in range(6):
            at = 2 * f * block_x
            low, high = message[j, at : at + block_x], message[j, at + block_x : at + 2 * block_x]
            got.append(jnp.concatenate([low, high], axis=1))
        return other(got[:5], jnp.where(inside, got[5], 0.0))

    bottom = face(1, arrived(jnp.maximum(col - 1, 0), col > 0), edge(0))
    top = face(1, edge(block_y - 1), arrived(jnp.minimum(col + 1, cols - 1), col < cols - 1))
    row = lax.broadcasted_iota(I32, (TILE, block_z), 0)

    def corrected(i, x, t):
        at = slice(t * TILE, (t + 1) * TILE)
        value = most[i, x, at]
        if t == 0:
            value = value + jnp.where(row == 0, scale_ref[x, at] * bottom[i][x : x + 1], 0.0)
        if t == tiles - 1:
            value = value - jnp.where(row == TILE - 1, scale_ref[x, at] * top[i][x : x + 1], 0.0)
        return value

    for t in (0, tiles - 1):
        at = slice(t * TILE, (t + 1) * TILE)
        for x in range(block_x):
            for i in range(4):
                state[i, x, at] = corrected(i, x, t)
        send(state.at[0:4, :, at], state_out.at[0:4, :, at])
    for k in range(3):
        own = new[QUARTERS * k : QUARTERS * k + 1]
        for j in range(1, cols):
            at = QUARTERS * k + j
            own = jnp.where(col == j, new[at : at + 1], own)
        own_motion[k] = own
    send(own_motion, motion_out)
    for x in range(block_x):
        for t in range(tiles):
            at = slice(t * TILE, (t + 1) * TILE)
            first = x * block_y + t * TILE
            state[4, x, at] = corrected(4, x, t) + scale_ref[x, at] * found[first : first + TILE]
    send(state.at[4], state_out.at[4])
    for copy in copies:
        copy.wait()


def in_vmem(*arrays):
    return [pltpu.with_memory_space_constraint(array, pltpu.VMEM) for array in arrays]


def in_hbm(*arrays):
    return [pltpu.with_memory_space_constraint(array, pltpu.HBM) for array in arrays]


def local(
    density,
    velocity,
    pressure,
    fraction_code,
    interface_cell,
    interface_element,
    interface_count,
    wall_normal,
    element_mass,
    element_removed,
    element_velocity,
):
    block_x, block_y, block_z = density.shape
    rows = interface_cell.shape[2]
    group = element_mass.shape[1]
    slabs, cols = lax.axis_size("slab"), lax.axis_size("col")
    share = group // cols
    vmem = pl.BlockSpec(memory_space=pltpu.VMEM)
    hbm = pl.BlockSpec(memory_space=pltpu.HBM)
    given = (
        density,
        velocity,
        pressure,
        fraction_code,
        wall_normal,
        element_mass,
        element_removed,
        element_velocity,
    )
    results = pl.pallas_call(
        gather_kernel,
        out_shape=tuple(pltpu.VMEM(array.shape, array.dtype) for array in given)
        + (
            jax.ShapeDtypeStruct((cols, MESSAGE_ROWS, LANES), F32),
            pltpu.VMEM((1, rows), F32),
            pltpu.VMEM((block_z, rows), BF16),
            pltpu.VMEM((block_x * block_y, rows), BF16),
            pltpu.VMEM((LANES, rows), BF16),
            pltpu.VMEM((16, rows), F32),
        ),
        in_specs=[pl.BlockSpec(memory_space=pl.ANY)] + [hbm] * 10,
        out_specs=[vmem] * 8 + [hbm] + [vmem] * 5,
        scratch_shapes=[
            pltpu.VMEM(interface_count.shape, I32),
            pltpu.VMEM(interface_cell.shape, I32),
            pltpu.VMEM(interface_element.shape, I32),
            pltpu.VMEM((cols, MESSAGE_ROWS, LANES), F32),
            pltpu.SemaphoreType.DMA((11,)),
            pltpu.SemaphoreType.DMA((2,)),
        ],
        compiler_params=pltpu.CompilerParams(vmem_limit_bytes=VMEM_BYTES),
        name="gather_rows",
    )(
        interface_count,
        *in_hbm(interface_cell, interface_element, *given),
    )
    kept, message, hots = results[:8], results[8], results[9:]

    message_in = lax.all_to_all(
        message, "col", 0, 0, axis_index_groups=[list(ORDER)]
    )
    planes = pltpu.VMEM((6, block_y, block_z), F32)
    far, near = pl.pallas_call(
        plane_kernel,
        out_shape=(planes, planes),
        in_specs=[vmem] * 4,
        out_specs=[vmem] * 2,
        cost_estimate=pl.CostEstimate(flops=100000, bytes_accessed=100000, transcendentals=0),
        compiler_params=pltpu.CompilerParams(vmem_limit_bytes=VMEM_BYTES),
        name="pack_planes",
    )(*in_vmem(*kept[:4]))
    pushed, total, terms, elements = pl.pallas_call(
        inner_kernel,
        out_shape=(
            pltpu.VMEM((3, block_x, block_y, block_z), F32),
            pltpu.VMEM((5, block_x, block_y, block_z), F32),
            pltpu.VMEM((5, block_x, block_y, block_z), F32),
            pltpu.VMEM((3, 16, LANES), F32),
        ),
        in_specs=[vmem] * 11,
        out_specs=[vmem] * 4,
        cost_estimate=pl.CostEstimate(flops=10000000000, bytes_accessed=100000000, transcendentals=0),
        compiler_params=pltpu.CompilerParams(vmem_limit_bytes=VMEM_BYTES),
        name="inner_faces",
    )(*in_vmem(*kept, *hots[:3]))
    inner = [(i, i ^ 1) for i in range(slabs)]
    outer = [(i, i + 1 if i % 2 else i - 1) for i in range(1, slabs - 1)]
    far_in = lax.ppermute(far, "slab", outer)
    near_in = lax.ppermute(near, "slab", inner)

    cells = in_vmem(*kept[:4])
    most, scale = pl.pallas_call(
        outer_kernel,
        out_shape=(
            pltpu.VMEM((5, block_x, block_y, block_z), F32),
            pltpu.VMEM((block_x, block_y, block_z), F32),
        ),
        in_specs=[vmem] * 9,
        out_specs=[vmem] * 2,
        cost_estimate=pl.CostEstimate(
            flops=100 * density.size, bytes_accessed=64 * density.size, transcendentals=0
        ),
        compiler_params=pltpu.CompilerParams(vmem_limit_bytes=VMEM_BYTES),
        name="outer_faces",
    )(*cells, *in_vmem(pushed, total, terms, far_in, near_in))
    state, new_motion = pl.pallas_call(
        step_kernel,
        out_shape=(
            jax.ShapeDtypeStruct((5, block_x, block_y, block_z), F32),
            jax.ShapeDtypeStruct((3, 1, share), F32),
        ),
        in_specs=[vmem] * 14,
        out_specs=[hbm, hbm],
        scratch_shapes=[
            pltpu.VMEM((5, block_x, block_y, block_z), F32),
            pltpu.VMEM((3, 1, share), F32),
            pltpu.SemaphoreType.DMA((5,)),
        ],
        compiler_params=pltpu.CompilerParams(vmem_limit_bytes=VMEM_BYTES),
        name="step_cells",
    )(*in_vmem(*kept[:4], terms, elements, most, scale, message_in, *hots))
    return (state, new_motion)


def solution(mesh):
    placed = (
        P("slab", "col", None),
        P(None, "slab", "col", None),
        P("slab", "col", None),
        P("slab", "col", None),
        P("slab", "col", None),
        P("slab", "col", None),
        P("slab", "col"),
        P(None, "slab", "col", None),
        P("slab", None),
        P("slab", None),
        P(None, "slab", None),
    )
    return jax.shard_map(
        local,
        mesh=mesh,
        in_specs=placed,
        out_specs=(P(None, "slab", "col", None), P(None, "slab", "col")),
        check_vma=False,
    )
```

```python
import jax
import jax.numpy as jnp
from jax import lax
from jax.experimental import pallas as pl
from jax.experimental.pallas import tpu as pltpu
from jax.sharding import PartitionSpec as P

ratio_heat = 1.4
step_ratio = 0.1
struct_step = 1.0

F32, BF16, I32 = jnp.float32, jnp.bfloat16, jnp.int32
ORDER = (0, 2, 3, 1)
VMEM_BYTES = 8 * 2**20
TILE = 8
LANES = 128
LOADS_AT = 24
MESSAGE_ROWS = 40
QUARTERS = 4


def split3(value):
    high = value.astype(BF16).astype(F32)
    rest = value - high
    middle = rest.astype(BF16).astype(F32)
    return high, middle, rest - middle


def gather_kernel(count_in, cell_in, element_in, *refs):
    given, kept = refs[:5], refs[5:10]
    message_out, weight_ref, third_hot, plane_hot, low_hot, pull_ref = refs[10:16]
    count, cell, element, message, sems, sent = refs[16:]
    density, velocity, pressure, code, normal = kept[:5]
    pairs = [(cell_in, cell), (element_in, element), (count_in, count)]
    pairs += [(given[i], kept[i]) for i in (2, 3, 4, 0, 1)]
    copies = [pltpu.make_async_copy(a, b, sems.at[i]) for i, (a, b) in enumerate(pairs)]
    for copy in copies:
        copy.start()
    block_x, block_y, block_z = density.shape
    rows = cell.shape[2]
    col = lax.axis_index("col")

    copies[0].wait()
    copies[1].wait()
    place = cell[0]
    third = jnp.bitwise_and(place, block_z - 1)
    plane = lax.shift_right_logical(place, block_z.bit_length() - 1)
    third_mask = lax.broadcasted_iota(I32, (block_z, rows), 0) == third
    third_hot[...] = jnp.where(third_mask, 1.0, 0.0).astype(BF16)
    plane_mask = lax.broadcasted_iota(I32, (block_x * block_y, rows), 0) == plane
    plane_hot[...] = jnp.where(plane_mask, 1.0, 0.0).astype(BF16)
    low_mask = lax.broadcasted_iota(I32, (LANES, rows), 0) == jnp.bitwise_and(element[0], LANES - 1)
    low_hot[...] = jnp.where(low_mask, 1.0, 0.0).astype(BF16)
    for copy in copies[2:6]:
        copy.wait()
    line = lax.broadcasted_iota(I32, (16, rows), 0)
    high = lax.shift_right_logical(element[0], LANES.bit_length() - 1)
    pull = jnp.zeros((16, rows), F32)
    for k in range(3):
        pull = jnp.where(line == high + QUARTERS * k, normal[k, 0], pull)
    pull_ref[...] = pull
    fraction = code[...].astype(F32) * (1.0 / 16.0)
    table = (pressure[...] * (1.0 - fraction)).reshape(block_x * block_y, block_z)
    parts = jnp.concatenate(split3(table), axis=0).astype(BF16)
    found = jnp.dot(parts, third_hot[...], preferred_element_type=F32)
    n = block_x * block_y
    found = found[:n] + found[n : 2 * n] + found[2 * n :]
    found = jnp.sum(jnp.where(plane_mask, found, 0.0), axis=0, keepdims=True)
    live = lax.broadcasted_iota(I32, (1, rows), 1) < count[...]
    weight = jnp.where(live, found, 0.0)
    weight_ref[...] = weight

    for copy in copies[6:]:
        copy.wait()
    def edge(x, y):
        out = [density[x, y : y + 1]]
        out += [velocity[k, x, y : y + 1] for k in range(3)]
        out += [pressure[x, y : y + 1], code[x, y : y + 1].astype(F32) * (1.0 / 16.0)]
        return out

    for x in range(block_x):
        first, last = edge(x, 0), edge(x, block_y - 1)
        for j in range(message.shape[0]):
            for f in range(6):
                row = jnp.where(col < ORDER[j], last[f], first[f])
                for h in range(2):
                    at = (2 * f + h) * block_x + x
                    message[j, at : at + 1] = row[:, h * LANES : (h + 1) * LANES]
    edges = slice(0, LOADS_AT)
    edge_copy = pltpu.make_async_copy(message.at[:, edges], message_out.at[:, edges], sent.at[0])
    edge_copy.start()

    force = jnp.concatenate(split3(-weight * pull), axis=0).astype(BF16)
    partial = lax.dot_general(
        force, low_hot[...], (((1,), (1,)), ((), ())), preferred_element_type=F32
    )
    partial = partial[:16] + partial[16:32] + partial[32:]
    for j in range(message.shape[0]):
        message[j, LOADS_AT:] = partial
    loads = slice(LOADS_AT, MESSAGE_ROWS)
    load_copy = pltpu.make_async_copy(message.at[:, loads], message_out.at[:, loads], sent.at[1])
    load_copy.start()
    edge_copy.wait()
    load_copy.wait()


def derive(density, v0, v1, v2, pressure):
    m0, m1, m2 = density * v0, density * v1, density * v2
    energy = pressure * (1.0 / 0.4) + 0.5 * density * (v0 * v0 + v1 * v1 + v2 * v2)
    sound = jnp.sqrt(ratio_heat * pressure / density)
    return m0, m1, m2, energy, sound


RHO, V0, V1, V2, PRS, FRAC, M0, M1, M2, ENE, SND = range(11)


def face(along, low, high):
    vl, vh = low[V0 + along], high[V0 + along]
    speed = jnp.maximum(jnp.abs(vl) + low[SND], jnp.abs(vh) + high[SND])
    half = 0.5 * jnp.minimum(low[FRAC], high[FRAC])
    out = []
    for i, name in enumerate((RHO, M0, M1, M2, ENE)):
        if name == RHO:
            both = low[M0 + along] + high[M0 + along]
        elif name == ENE:
            both = vl * (low[ENE] + low[PRS]) + vh * (high[ENE] + high[PRS])
        else:
            both = vl * low[name] + vh * high[name]
            if i == 1 + along:
                both = both + (low[PRS] + high[PRS])
        out.append(half * (both - speed * (high[name] - low[name])))
    return out


def plane_kernel(density, velocity, pressure, code, far_ref, near_ref):
    odd = lax.rem(lax.axis_index("slab"), 2)
    for target, at in ((far_ref, odd), (near_ref, 1 - odd)):
        target[0] = density[at]
        for k in range(3):
            target[1 + k] = velocity[k, at]
        target[4] = pressure[at]
        target[5] = code[at].astype(F32) * (1.0 / 16.0)


def scatter(hot, third_hot, row):
    left = jnp.concatenate([hot * part.astype(BF16) for part in split3(row)], axis=0)
    found = lax.dot_general(
        left, third_hot[...], (((1,), (1,)), ((), ())), preferred_element_type=F32
    )
    n = hot.shape[0]
    return found[:n] + found[n : 2 * n] + found[2 * n :]


def inner_kernel(
    density,
    velocity,
    pressure,
    code,
    normal,
    mass_in,
    removed_in,
    motion_in,
    weight,
    third_hot,
    plane_hot,
    source,
    total,
    terms,
    element,
    mass,
    removed,
    motion,
    sems,
):
    pairs = ((mass_in, mass), (removed_in, removed), (motion_in, motion))
    copies = [pltpu.make_async_copy(a, b, sems.at[i]) for i, (a, b) in enumerate(pairs)]
    for copy in copies:
        copy.start()
    hot = plane_hot[...]
    for k in range(3):
        source[k] = scatter(hot, third_hot, weight[...] * normal[k, 0]).reshape(density.shape)
    block_x, block_y, block_z = density.shape
    lane = lax.broadcasted_iota(I32, (TILE, block_z), 1)
    row = lax.broadcasted_iota(I32, (TILE, block_z), 0)
    tiles = block_y // TILE

    def prims(x, t):
        at = slice(t * TILE, (t + 1) * TILE)
        out = [density[x, at]] + [velocity[k, x, at] for k in range(3)]
        return out + [pressure[x, at], code[x, at].astype(F32) * (1.0 / 16.0)]

    def shifted(value, after):
        return jnp.where(row == TILE - 1, pltpu.roll(after, TILE - 1, 0), pltpu.roll(value, TILE - 1, 0))

    def full(x, t):
        own = prims(x, t)
        return dict(enumerate(own + list(derive(*own[:5]))))

    def keep(x, t, own):
        at = slice(t * TILE, (t + 1) * TILE)
        for i, name in enumerate((M0, M1, M2, ENE, SND)):
            terms[i, x, at] = own[name]

    for t in range(tiles):
        low, high = full(0, t), full(1, t)
        keep(0, t, low)
        keep(1, t, high)
        across = face(0, low, high)
        at = slice(t * TILE, (t + 1) * TILE)
        for x, own in ((0, low), (1, high)):
            right = {name: pltpu.roll(value, block_z - 1, 1) for name, value in own.items()}
            right[FRAC] = jnp.where(lane == block_z - 1, 0.0, right[FRAC])
            upper = face(2, own, right)
            for i in range(5):
                value = upper[i] - pltpu.roll(upper[i], 1, 1)
                total[i, x, at] = value + across[i] if x == 0 else value - across[i]
    for x in range(block_x):
        before = None
        for t in range(tiles):
            at = slice(t * TILE, (t + 1) * TILE)

            def load(u):
                at = slice(u * TILE, (u + 1) * TILE)
                out = {RHO: density[x, at], V1: velocity[1, x, at], PRS: pressure[x, at]}
                out[FRAC] = code[x, at].astype(F32) * (1.0 / 16.0)
                for i, name in enumerate((M0, M1, M2, ENE, SND)):
                    out[name] = terms[i, x, at]
                return out

            own = load(t)
            after = load(min(t + 1, tiles - 1))
            above = {name: shifted(own[name], after[name]) for name in own}
            if t == tiles - 1:
                above[FRAC] = jnp.where(row == TILE - 1, 0.0, above[FRAC])
            upper = face(1, own, above)
            turned = [pltpu.roll(value, 1, 0) for value in upper]
            for i in range(5):
                first = jnp.zeros_like(turned[i]) if before is None else before[i]
                total[i, x, at] += upper[i] - jnp.where(row == 0, first, turned[i])
            before = turned
    for copy in copies:
        copy.wait()
    element[...] = jnp.ones_like(element)
    for q in range(QUARTERS):
        at = slice(q * LANES, (q + 1) * LANES)
        kept = 1.0 - removed[:, at].astype(F32)
        for k in range(3):
            line = slice(QUARTERS * k + q, QUARTERS * k + q + 1)
            element[0, line] = struct_step / mass[:, at]
            element[1, line] = kept
            element[2, line] = motion[k, :, at]


def other(prims, fraction):
    live = fraction > 0.0
    prims = [jnp.where(live, prims[0], 1.0)] + prims[1:4] + [jnp.where(live, prims[4], 1.0)]
    return dict(enumerate(prims + [fraction] + list(derive(*prims))))


def outer_kernel(
    density, velocity, pressure, code, pushed, total, terms, far_ref, near_ref, most, scale_ref
):
    block_x, block_y, block_z = density.shape
    odd = lax.rem(lax.axis_index("slab"), 2)
    for x in range(block_x):
        use_near = odd == (1 - x)
        for t in range(block_y // TILE):
            at = slice(t * TILE, (t + 1) * TILE)
            got = [jnp.where(use_near, near_ref[f, at], far_ref[f, at]) for f in range(6)]
            beyond = other(got[:5], got[5])
            own = {RHO: density[x, at], PRS: pressure[x, at], V0: velocity[0, x, at]}
            for k in range(3):
                own[M0 + k] = terms[k, x, at]
            own[FRAC] = code[x, at].astype(F32) * (1.0 / 16.0)
            own[ENE], own[SND] = terms[3, x, at], terms[4, x, at]
            flux = face(0, beyond, own) if x == 0 else face(0, own, beyond)
            scale = step_ratio / own[FRAC]
            scale_ref[x, at] = scale
            for i, name in enumerate((RHO, M0, M1, M2, ENE)):
                change = total[i, x, at] - flux[i] if x == 0 else total[i, x, at] + flux[i]
                if 0 < i < 4:
                    change = change - pushed[i - 1, x, at]
                most[i, x, at] = own[name] - scale * change


def step_kernel(
    density,
    velocity,
    pressure,
    code,
    terms,
    element,
    most,
    scale_ref,
    message,
    weight_ref,
    third_hot,
    plane_hot,
    low_hot,
    pull_ref,
    state_out,
    motion_out,
    state,
    own_motion,
    sems,
):
    block_x, block_y, block_z = density.shape
    cols = message.shape[0]
    col = lax.axis_index("col")
    tiles = block_y // TILE
    copies = []

    def send(source, target):
        copies.append(pltpu.make_async_copy(source, target, sems.at[len(copies)]))
        copies[-1].start()

    at = slice(TILE, block_y - TILE)
    send(most.at[0:4, :, at], state_out.at[0:4, :, at])

    rows = slice(LOADS_AT, MESSAGE_ROWS)
    loads = message[0, rows]
    for j in range(1, cols):
        loads = loads + message[j, rows]
    new = (element[2] + loads * element[0]) * element[1]
    parts = jnp.concatenate(split3(new), axis=0).astype(BF16)
    moved = jnp.dot(parts, low_hot[...], preferred_element_type=F32)
    moved = moved[:16] + moved[16:32] + moved[32:]
    work = jnp.sum(pull_ref[...] * moved, axis=0, keepdims=True)
    found = scatter(plane_hot[...], third_hot, weight_ref[...] * work)

    def edge(along_y):
        out = {RHO: density[:, along_y], PRS: pressure[:, along_y]}
        for k in range(3):
            out[V0 + k] = velocity[k, :, along_y]
            out[M0 + k] = terms[k, :, along_y]
        out[FRAC] = code[:, along_y].astype(F32) * (1.0 / 16.0)
        out[ENE], out[SND] = terms[3, :, along_y], terms[4, :, along_y]
        return out

    def arrived(beside, inside):
        j = sum(jnp.where(beside == c, place, 0) for place, c in enumerate(ORDER))
        got = []
        for f in range(6):
            at = 2 * f * block_x
            low, high = message[j, at : at + block_x], message[j, at + block_x : at + 2 * block_x]
            got.append(jnp.concatenate([low, high], axis=1))
        return other(got[:5], jnp.where(inside, got[5], 0.0))

    bottom = face(1, arrived(jnp.maximum(col - 1, 0), col > 0), edge(0))
    top = face(1, edge(block_y - 1), arrived(jnp.minimum(col + 1, cols - 1), col < cols - 1))
    row = lax.broadcasted_iota(I32, (TILE, block_z), 0)

    def corrected(i, x, t):
        at = slice(t * TILE, (t + 1) * TILE)
        value = most[i, x, at]
        if t == 0:
            value = value + jnp.where(row == 0, scale_ref[x, at] * bottom[i][x : x + 1], 0.0)
        if t == tiles - 1:
            value = value - jnp.where(row == TILE - 1, scale_ref[x, at] * top[i][x : x + 1], 0.0)
        return value

    for t in (0, tiles - 1):
        at = slice(t * TILE, (t + 1) * TILE)
        for x in range(block_x):
            for i in range(4):
                state[i, x, at] = corrected(i, x, t)
        send(state.at[0:4, :, at], state_out.at[0:4, :, at])
    for k in range(3):
        own = new[QUARTERS * k : QUARTERS * k + 1]
        for j in range(1, cols):
            at = QUARTERS * k + j
            own = jnp.where(col == j, new[at : at + 1], own)
        own_motion[k] = own
    send(own_motion, motion_out)
    for x in range(block_x):
        for t in range(tiles):
            at = slice(t * TILE, (t + 1) * TILE)
            first = x * block_y + t * TILE
            state[4, x, at] = corrected(4, x, t) + scale_ref[x, at] * found[first : first + TILE]
    send(state.at[4], state_out.at[4])
    for copy in copies:
        copy.wait()


def in_vmem(*arrays):
    return [pltpu.with_memory_space_constraint(array, pltpu.VMEM) for array in arrays]


def in_hbm(*arrays):
    return [pltpu.with_memory_space_constraint(array, pltpu.HBM) for array in arrays]


def local(
    density,
    velocity,
    pressure,
    fraction_code,
    interface_cell,
    interface_element,
    interface_count,
    wall_normal,
    element_mass,
    element_removed,
    element_velocity,
):
    block_x, block_y, block_z = density.shape
    rows = interface_cell.shape[2]
    group = element_mass.shape[1]
    slabs, cols = lax.axis_size("slab"), lax.axis_size("col")
    share = group // cols
    vmem = pl.BlockSpec(memory_space=pltpu.VMEM)
    hbm = pl.BlockSpec(memory_space=pltpu.HBM)
    given = (
        density,
        velocity,
        pressure,
        fraction_code,
        wall_normal,
    )
    results = pl.pallas_call(
        gather_kernel,
        out_shape=tuple(pltpu.VMEM(array.shape, array.dtype) for array in given)
        + (
            jax.ShapeDtypeStruct((cols, MESSAGE_ROWS, LANES), F32),
            pltpu.VMEM((1, rows), F32),
            pltpu.VMEM((block_z, rows), BF16),
            pltpu.VMEM((block_x * block_y, rows), BF16),
            pltpu.VMEM((LANES, rows), BF16),
            pltpu.VMEM((16, rows), F32),
        ),
        in_specs=[pl.BlockSpec(memory_space=pl.ANY)] + [hbm] * 7,
        out_specs=[vmem] * 5 + [hbm] + [vmem] * 5,
        scratch_shapes=[
            pltpu.VMEM(interface_count.shape, I32),
            pltpu.VMEM(interface_cell.shape, I32),
            pltpu.VMEM(interface_element.shape, I32),
            pltpu.VMEM((cols, MESSAGE_ROWS, LANES), F32),
            pltpu.SemaphoreType.DMA((8,)),
            pltpu.SemaphoreType.DMA((2,)),
        ],
        compiler_params=pltpu.CompilerParams(vmem_limit_bytes=VMEM_BYTES),
        name="gather_rows",
    )(
        interface_count,
        *in_hbm(interface_cell, interface_element, *given),
    )
    kept, message, hots = results[:5], results[5], results[6:]

    message_in = lax.all_to_all(
        message, "col", 0, 0, axis_index_groups=[list(ORDER)]
    )
    planes = pltpu.VMEM((6, block_y, block_z), F32)
    far, near = pl.pallas_call(
        plane_kernel,
        out_shape=(planes, planes),
        in_specs=[vmem] * 4,
        out_specs=[vmem] * 2,
        cost_estimate=pl.CostEstimate(flops=100000, bytes_accessed=100000, transcendentals=0),
        compiler_params=pltpu.CompilerParams(vmem_limit_bytes=VMEM_BYTES),
        name="pack_planes",
    )(*in_vmem(*kept[:4]))
    pushed, total, terms, elements = pl.pallas_call(
        inner_kernel,
        out_shape=(
            pltpu.VMEM((3, block_x, block_y, block_z), F32),
            pltpu.VMEM((5, block_x, block_y, block_z), F32),
            pltpu.VMEM((5, block_x, block_y, block_z), F32),
            pltpu.VMEM((3, 16, LANES), F32),
        ),
        in_specs=[vmem] * 5 + [hbm] * 3 + [vmem] * 3,
        out_specs=[vmem] * 4,
        scratch_shapes=[
            pltpu.VMEM(element_mass.shape, F32),
            pltpu.VMEM(element_removed.shape, I32),
            pltpu.VMEM(element_velocity.shape, F32),
            pltpu.SemaphoreType.DMA((3,)),
        ],
        cost_estimate=pl.CostEstimate(flops=10000000000, bytes_accessed=100000000, transcendentals=0),
        compiler_params=pltpu.CompilerParams(vmem_limit_bytes=VMEM_BYTES),
        name="inner_faces",
    )(
        *in_vmem(*kept),
        *in_hbm(element_mass, element_removed, element_velocity),
        *in_vmem(*hots[:3]),
    )
    inner = [(i, i ^ 1) for i in range(slabs)]
    outer = [(i, i + 1 if i % 2 else i - 1) for i in range(1, slabs - 1)]
    far_in = lax.ppermute(far, "slab", outer)
    near_in = lax.ppermute(near, "slab", inner)

    cells = in_vmem(*kept[:4])
    most, scale = pl.pallas_call(
        outer_kernel,
        out_shape=(
            pltpu.VMEM((5, block_x, block_y, block_z), F32),
            pltpu.VMEM((block_x, block_y, block_z), F32),
        ),
        in_specs=[vmem] * 9,
        out_specs=[vmem] * 2,
        cost_estimate=pl.CostEstimate(
            flops=100 * density.size, bytes_accessed=64 * density.size, transcendentals=0
        ),
        compiler_params=pltpu.CompilerParams(vmem_limit_bytes=VMEM_BYTES),
        name="outer_faces",
    )(*cells, *in_vmem(pushed, total, terms, far_in, near_in))
    state, new_motion = pl.pallas_call(
        step_kernel,
        out_shape=(
            jax.ShapeDtypeStruct((5, block_x, block_y, block_z), F32),
            jax.ShapeDtypeStruct((3, 1, share), F32),
        ),
        in_specs=[vmem] * 14,
        out_specs=[hbm, hbm],
        scratch_shapes=[
            pltpu.VMEM((5, block_x, block_y, block_z), F32),
            pltpu.VMEM((3, 1, share), F32),
            pltpu.SemaphoreType.DMA((5,)),
        ],
        compiler_params=pltpu.CompilerParams(vmem_limit_bytes=VMEM_BYTES),
        name="step_cells",
    )(*in_vmem(*kept[:4], terms, elements, most, scale, message_in, *hots))
    return (state, new_motion)


def solution(mesh):
    placed = (
        P("slab", "col", None),
        P(None, "slab", "col", None),
        P("slab", "col", None),
        P("slab", "col", None),
        P("slab", "col", None),
        P("slab", "col", None),
        P("slab", "col"),
        P(None, "slab", "col", None),
        P("slab", None),
        P("slab", None),
        P(None, "slab", None),
    )
    return jax.shard_map(
        local,
        mesh=mesh,
        in_specs=placed,
        out_specs=(P(None, "slab", "col", None), P(None, "slab", "col")),
        check_vma=False,
    )
```
